512 devices in a mesh: seg: 8 (over x, core), state: 64 (over z, y).
Axes of the slice: x: 4, y: 8, z: 8, core: 2. Of those that a mesh axis runs over, the one named last changes fastest.
Arguments:
- forward_in: float32 [8, 8388608], P('seg', 'state'), may hold values from 0.3 to 28, as said below
- backward_in: float32 [8, 8388608], P('seg', 'state'), may hold values from 0.3 to 28, as said below
- compat_masks: int32 [16, 23], P('seg'), may hold values from 1 to 3
- theta_index: int32 [16, 23], P('seg'), may hold values from 0 to 5
Outputs:
- forward_out: float32 [8, 8388608], P('seg', 'state')
- backward_out: float32 [8, 8388608], P('seg', 'state')
- posterior: float32 [8, 8388608], P('seg', 'state')
- log_scales: float32 [2, 8], P(None, 'seg')
The draws below stay inside these ranges and needn't reach their ends.
Inputs may be any that keep to these rules, and one draw needn't show every extreme that they name: `compat_masks`: 1 allows anchor 0 only, 2 anchor 1 only, 3 both. `forward_in`: positive. `backward_in`: positive.
All inputs are finite; a program needn't handle non-finite values.
Results may differ from the reference program's by a relative error of at most 0.00011.
Values sent between devices are 32-bit elements; how exact they have to be, the bound alone decides.
No kernel may reach another device: no remote copies, remote signals or barrier semaphores. Data moves between devices by JAX's collectives and lax.ppermute only.
A program may use at most 64 MiB of HBM per device.

```python
import jax
import jax.numpy as jnp
from jax import lax

MEIOSES = 23
STATES = 8388608
SEGS = 8
MARKERS = 16


def message_draw(key, salt):
    stream = jax.random.fold_in(key, salt)
    position = jnp.arange(STATES, dtype=jnp.float32) / STATES
    rising = 10.0 ** position
    noise_part = jax.random.uniform(stream, (SEGS, STATES), jnp.float32, -1.0, 1.0)
    return rising[None, :] * jnp.exp(noise_part)


def draw_forward_in(key, part):
    return message_draw(key, 11)


def draw_backward_in(key, part):
    return message_draw(key, 23)


def plant(values, rng, smallest, high):
    spot = [jax.random.randint(jax.random.fold_in(rng, axis), (), 0, length) for axis, length in enumerate(values.shape)]
    main_axis = values.shape.index(max(values.shape))
    neighbour = spot[:main_axis] + [(spot[main_axis] + 1) % values.shape[main_axis]] + spot[main_axis + 1:]
    return values.at[tuple(spot)].set(smallest).at[tuple(neighbour)].set(high)


def setup_inputs(seed: int = 0) -> dict:
    arg_keys = jax.random.split(jax.random.key(seed), 5)
    forward_in = draw_forward_in(jax.random.fold_in(arg_keys[4], 71), 0)
    backward_in = draw_backward_in(jax.random.fold_in(arg_keys[4], 71), 0)
    compat_masks = plant(jax.random.randint(arg_keys[2], (MARKERS, MEIOSES), 1, 4), jax.random.fold_in(arg_keys[2], 1), 1, 3).astype(jnp.int32)
    theta_index = plant(jax.random.randint(arg_keys[3], (MARKERS, MEIOSES), 0, 6), jax.random.fold_in(arg_keys[3], 1), 0, 5).astype(jnp.int32)
    return {"forward_in": forward_in, "backward_in": backward_in, "compat_masks": compat_masks, "theta_index": theta_index}


PENALTY = 0.5
ERROR_RATE = 0.02
BASE_THETA = 0.01


def theta_table(theta_index):
    return BASE_THETA * 2.0 ** theta_index.astype(jnp.float32)


def kron_matrix(thetas):
    count = thetas.shape[0]
    width = 2 ** count
    row_ids = lax.broadcasted_iota(jnp.int32, (width, width), 0)
    col_ids = lax.broadcasted_iota(jnp.int32, (width, width), 1)
    result = jnp.ones((width, width), jnp.float32)
    for which in range(count):
        agrees = (row_ids // 2 ** which) % 2 == (col_ids // 2 ** which) % 2
        result = result * jnp.where(agrees, 1.0 - thetas[which], thetas[which])
    return result


def mix_all(vector, thetas):
    count = thetas.shape[0]
    offset = 0
    current = vector
    while offset < count:
        width_bits = min(4, count - offset)
        shaped = current.reshape(-1, 2 ** width_bits, 2 ** offset)
        current = jnp.einsum("ij,ojk->oik", kron_matrix(thetas[offset:offset + width_bits]), shaped,
                             precision=lax.Precision.HIGHEST).reshape(-1)
        offset += width_bits
    return current


def emission_full(mask_row):
    count = mask_row.shape[0]
    anchor_zero = jnp.where(mask_row % 2 == 1, 1.0, PENALTY).astype(jnp.float32)
    anchor_one = jnp.where(mask_row // 2 == 1, 1.0, PENALTY).astype(jnp.float32)
    product = jnp.ones((1,), jnp.float32)
    for which in range(count):
        pair = jnp.stack([anchor_zero[which], anchor_one[which]])
        product = (pair[:, None] * product[None, :]).reshape(-1)
    return ERROR_RATE + (1.0 - ERROR_RATE) * product


def reference(forward_in, backward_in, compat_masks, theta_index):
    thetas = theta_table(theta_index)
    segments = forward_in.shape[0]
    per_segment = compat_masks.shape[0] // segments
    forwards = []
    backwards = []
    log_fwd = []
    log_bwd = []
    for segment in range(segments):
        forward = forward_in[segment]
        total_log = jnp.zeros((), jnp.float32)
        for offset in range(per_segment):
            marker = segment * per_segment + offset
            update = emission_full(compat_masks[marker]) * mix_all(forward, thetas[marker])
            scale = jnp.mean(update)
            forward = update / scale
            total_log = total_log + jnp.log(scale)
        forwards.append(forward)
        log_fwd.append(total_log)
        backward = backward_in[segment]
        total_log = jnp.zeros((), jnp.float32)
        for offset in range(per_segment - 1, -1, -1):
            marker = segment * per_segment + offset
            update = mix_all(emission_full(compat_masks[marker]) * backward, thetas[marker])
            scale = jnp.mean(update)
            backward = update / scale
            total_log = total_log + jnp.log(scale)
        backwards.append(backward)
        log_bwd.append(total_log)
    posts = []
    for segment in range(segments):
        if segment == 0:
            left_side = forward_in[0]
        else:
            left_side = forwards[segment - 1]
        product = left_side * backwards[segment]
        posts.append(product / jnp.mean(product))
    log_scales = jnp.stack([jnp.stack(log_fwd), jnp.stack(log_bwd)])
    return jnp.stack(forwards), jnp.stack(backwards), jnp.stack(posts), log_scales
```

```python
import jax
import jax.numpy as jnp
from jax import lax
from jax.experimental import pallas as pl
from jax.experimental.pallas import tpu as pltpu
from jax.sharding import PartitionSpec as P

PENALTY = 0.5
ERROR_RATE = 0.02
BASE_THETA = 0.01
LANE_BITS, LOW_BITS, SPLIT_BITS = 7, 11, 6
ROWS, LANES = 16, 128
MEIOSES = LOW_BITS + 2 * SPLIT_BITS
MID, HIGH = LOW_BITS, LOW_BITS + SPLIT_BITS
F32 = jnp.float32


def theta_list(theta_ref, marker):
    return [
        BASE_THETA * lax.shift_left(jnp.int32(1), theta_ref[marker, b]).astype(F32)
        for b in range(MEIOSES)
    ]


def anchor_list(mask_ref, marker):
    pairs = []
    for b in range(MEIOSES):
        mask = mask_ref[marker, b]
        zero = jnp.where(mask % 2 == 1, F32(1.0), F32(PENALTY))
        one = jnp.where(mask // 2 == 1, F32(1.0), F32(PENALTY))
        pairs.append((zero, one))
    return pairs


def lane_kron(thetas):
    differ = lax.broadcasted_iota(jnp.int32, (LANES, LANES), 0) ^ lax.broadcasted_iota(
        jnp.int32, (LANES, LANES), 1
    )
    result = jnp.ones((LANES, LANES), F32)
    for b in range(LANE_BITS):
        result = result * jnp.where((differ >> b) & 1 == 1, thetas[b], 1.0 - thetas[b])
    return result


def butterfly(values, thetas):
    values = list(values)
    for b, theta in enumerate(thetas):
        step = 1 << b
        for i in range(len(values)):
            if i & step == 0:
                moved = theta * (values[i + step] - values[i])
                values[i], values[i + step] = values[i] + moved, values[i + step] - moved
    return values


def mix_low(block, kron, thetas):
    block = jnp.dot(block, kron, precision=lax.Precision.HIGHEST, preferred_element_type=F32)
    block = block.reshape(-1, 8, LANES)
    row = lax.broadcasted_iota(jnp.int32, (1, 8, LANES), 1)
    for b in range(3):
        step = 1 << b
        other = pltpu.roll(block, step, axis=1)
        if step != 4:
            other = jnp.where((row >> b) & 1 == 1, other, pltpu.roll(block, 8 - step, axis=1))
        block = block + thetas[LANE_BITS + b] * (other - block)
    block = block.reshape(8, 2, 8, LANES)
    top, bottom = block[:, 0], block[:, 1]
    moved = thetas[10] * (bottom - top)
    top, bottom = top + moved, bottom - moved
    return [jnp.concatenate([top[j], bottom[j]], axis=0) for j in range(8)]


def low_factor(anchors):
    row = lax.broadcasted_iota(jnp.int32, (ROWS, LANES), 0)
    lane = lax.broadcasted_iota(jnp.int32, (ROWS, LANES), 1)
    position = row * LANES + lane
    result = jnp.full((ROWS, LANES), 1.0 - ERROR_RATE, F32)
    for b in range(LOW_BITS):
        zero, one = anchors[b]
        result = result * jnp.where((position >> b) & 1 == 1, one, zero)
    return result


def device_factor(anchors, first, device):
    result = F32(1.0)
    for b in range(SPLIT_BITS):
        zero, one = anchors[first + b]
        result = result * jnp.where((device >> b) & 1 == 1, one, zero)
    return result


def three_bits(anchors, first):
    factors = [None] * 8
    for i in range(8):
        value = anchors[first][i & 1]
        for b in (1, 2):
            value = value * anchors[first + b][(i >> b) & 1]
        factors[i] = value
    return factors


def emission_parts(mask_ref, marker, first_chunk, first_device, device):
    anchors = anchor_list(mask_ref, marker)
    own = device_factor(anchors, first_device, device)
    low = low_factor(anchors) * own
    inner = three_bits(anchors, first_chunk)
    outer = three_bits(anchors, first_chunk + 3)
    return outer, inner, low


def emitted(parts, i, j):
    outer, inner, low = parts
    return ERROR_RATE + (outer[i] * inner[j]) * low


def first_kernel(theta_ref, mask_ref, device_ref, fwd_ref, bwd_ref, out_ref, fwd_tmp, bwd_tmp):
    device = device_ref[0]
    for which, (source, tmp, marker) in enumerate(((fwd_ref, fwd_tmp, 0), (bwd_ref, bwd_tmp, 1))):
        thetas = theta_list(theta_ref, marker)
        kron = lane_kron(thetas)
        if which == 1:
            parts = emission_parts(mask_ref, 1, MID, HIGH, device)
        for i in range(8):
            block = source[pl.ds(i * 128, 128), :]
            if which == 1:
                block = jnp.concatenate(
                    [block[j * ROWS : (j + 1) * ROWS] * emitted(parts, i, j) for j in range(8)],
                    axis=0,
                )
            chunks = butterfly(mix_low(block, kron, thetas), thetas[MID : MID + 3])
            for j in range(8):
                tmp[8 * i + j] = chunks[j]
        for j in range(8):
            chunks = butterfly([tmp[8 * i + j] for i in range(8)], thetas[MID + 3 : HIGH])
            for i in range(8):
                out_ref[8 * i + j, pl.ds(which * ROWS, ROWS), :] = chunks[i]


def second_kernel(theta_ref, mask_ref, device_ref, in_ref, out_ref, tmp):
    device = device_ref[0]
    parts = emission_parts(mask_ref, 0, HIGH, MID, device)
    thetas = (theta_list(theta_ref, 0), theta_list(theta_ref, 1))
    kron = lane_kron(thetas[1])
    for which in range(2):
        before, after = thetas[which], thetas[1 - which]
        rows = pl.ds(which * ROWS, ROWS)
        for j in range(8):
            chunks = butterfly(
                [in_ref[8 * i + j, rows, :] for i in range(8)], before[HIGH + 3 : MEIOSES]
            )
            for i in range(8):
                tmp[8 * i + j] = chunks[i]
        for i in range(8):
            chunks = butterfly([tmp[8 * i + j] for j in range(8)], before[HIGH : HIGH + 3])
            chunks = [chunks[j] * emitted(parts, i, j) for j in range(8)]
            chunks = butterfly(chunks, after[HIGH : HIGH + 3])
            if which == 0:
                chunks = mix_low(jnp.concatenate(chunks, axis=0), kron, after)
            for j in range(8):
                tmp[8 * i + j] = chunks[j]
        for j in range(8):
            chunks = butterfly([tmp[8 * i + j] for i in range(8)], after[HIGH + 3 : MEIOSES])
            for i in range(8):
                out_ref[8 * i + j, rows, :] = chunks[i]


def forward_kernel(theta_ref, mask_ref, device_ref, in_ref, out_ref, sum_ref, tmp):
    device = device_ref[0]
    parts = emission_parts(mask_ref, 1, MID, HIGH, device)
    thetas = theta_list(theta_ref, 1)
    for i in range(8):
        chunks = butterfly(
            [in_ref[8 * i + j, pl.ds(0, ROWS), :] for j in range(8)], thetas[MID : MID + 3]
        )
        for j in range(8):
            tmp[8 * i + j] = chunks[j]
    acc = jnp.zeros((ROWS, LANES), F32)
    for j in range(8):
        chunks = butterfly([tmp[8 * i + j] for i in range(8)], thetas[MID + 3 : HIGH])
        for i in range(8):
            value = chunks[i] * emitted(parts, i, j)
            acc = acc + value
            out_ref[pl.ds((8 * i + j) * ROWS, ROWS), :] = value
    sum_ref[...] = acc[:8] + acc[8:]


def backward_kernel(theta_ref, in_ref, out_ref, sum_ref, tmp):
    thetas = theta_list(theta_ref, 0)
    kron = lane_kron(thetas)
    for i in range(8):
        block = jnp.concatenate(
            [in_ref[8 * i + j, pl.ds(ROWS, ROWS), :] for j in range(8)], axis=0
        )
        chunks = butterfly(mix_low(block, kron, thetas), thetas[MID : MID + 3])
        for j in range(8):
            tmp[8 * i + j] = chunks[j]
    acc = jnp.zeros((ROWS, LANES), F32)
    for j in range(8):
        chunks = butterfly([tmp[8 * i + j] for i in range(8)], thetas[MID + 3 : HIGH])
        for i in range(8):
            acc = acc + chunks[i]
            out_ref[pl.ds((8 * i + j) * ROWS, ROWS), :] = chunks[i]
    sum_ref[...] = acc[:8] + acc[8:]


def product_kernel(seg_ref, first_ref, got_ref, bwd_ref, fsum_ref, bsum_ref, out_ref, sum_ref):
    acc = jnp.zeros((8, LANES), F32)
    is_first = seg_ref[0] == 0
    for i in range(16):
        rows = pl.ds(64 * i, 64)
        left = jnp.where(is_first, first_ref[rows, :], got_ref[rows, :])
        value = left * bwd_ref[rows, :]
        out_ref[rows, :] = value
        acc = acc + jnp.sum(value.reshape(8, 8, LANES), axis=0)
    lane = lax.broadcasted_iota(jnp.int32, (1, LANES), 1)
    row = jnp.where(
        lane == 0,
        jnp.sum(fsum_ref[...]),
        jnp.where(lane == 1, jnp.sum(bsum_ref[...]), jnp.sum(acc)),
    )
    sum_ref[...] = jnp.broadcast_to(row[None], sum_ref.shape)


def scale_kernel(total_ref, fwd_ref, bwd_ref, post_ref, fwd_out, bwd_out, post_out, log_ref):
    totals = jnp.sum(total_ref[...], axis=0)
    means = totals * (1.0 / 2.0**MEIOSES)
    lane = lax.broadcasted_iota(jnp.int32, (1, LANES), 1)
    for which, (source, target) in enumerate(
        ((fwd_ref, fwd_out), (bwd_ref, bwd_out), (post_ref, post_out))
    ):
        mean = jnp.sum(jnp.where(lane == which, means, 0.0), axis=1, keepdims=True)
        scale = 1.0 / mean
        for i in range(8):
            rows = pl.ds(128 * i, 128)
            target[rows, :] = source[rows, :] * scale
        if which < 2:
            log_ref[pl.ds(which, 1), :] = jnp.log(mean)


SMEM = pl.BlockSpec(memory_space=pltpu.SMEM)
VMEM = pl.BlockSpec(memory_space=pltpu.VMEM)


def call(kernel, name, n_scalar, n_vector, outs, scratch=()):
    return pl.pallas_call(
        kernel,
        name=name,
        in_specs=[SMEM] * n_scalar + [VMEM] * n_vector,
        out_specs=[VMEM] * len(outs),
        out_shape=[jax.ShapeDtypeStruct(o, F32) for o in outs],
        scratch_shapes=[pltpu.VMEM(s, F32) for s in scratch],
    )


def exchanged(blocks):
    return lax.all_to_all(blocks, "state", split_axis=0, concat_axis=0, tiled=True)


def shards(forward_in, backward_in, compat_masks, theta_index):
    groups = lax.axis_size("state")
    chunk = (groups, ROWS, LANES)
    pair = (groups, 2 * ROWS, LANES)
    flat = (groups * ROWS, LANES)
    device = lax.axis_index("state").reshape(1)
    seg = lax.axis_index("seg").reshape(1)
    first = forward_in.reshape(flat)
    (both,) = call(first_kernel, "first", 3, 2, [pair], [chunk, chunk])(
        theta_index, compat_masks, device, first, backward_in.reshape(flat)
    )
    both = exchanged(both)
    (both,) = call(second_kernel, "second", 3, 1, [pair], [chunk])(
        theta_index, compat_masks, device, both
    )
    both = exchanged(both)
    forward, fsum = call(forward_kernel, "forward", 3, 1, [flat, (8, LANES)], [chunk])(
        theta_index, compat_masks, device, both
    )
    count = lax.axis_size("seg")
    received = lax.ppermute(forward, "seg", [(s, s + 1) for s in range(count - 1)])
    backward, bsum = call(backward_kernel, "backward", 1, 1, [flat, (8, LANES)], [chunk])(
        theta_index, both
    )
    product, sums = call(product_kernel, "product", 1, 5, [flat, (groups, 1, LANES)])(
        seg, first, received, backward, fsum, bsum
    )
    totals = exchanged(sums)
    forward, backward, posterior, logs = call(
        scale_kernel, "scale", 0, 4, [flat, flat, flat, (2, 1)]
    )(totals, forward, backward, product)
    return forward.reshape(1, -1), backward.reshape(1, -1), posterior.reshape(1, -1), logs


def solution(mesh):
    placed = (P("seg", "state"), P("seg", "state"), P("seg", None), P("seg", None))
    return jax.shard_map(
        shards,
        mesh=mesh,
        in_specs=placed,
        out_specs=(P("seg", "state"), P("seg", "state"), P("seg", "state"), P(None, "seg")),
        check_vma=False,
    )
```

```python
import jax
import jax.numpy as jnp
from jax import lax
from jax.experimental import pallas as pl
from jax.experimental.pallas import tpu as pltpu
from jax.sharding import PartitionSpec as P

PENALTY = 0.5
ERROR_RATE = 0.02
BASE_THETA = 0.01
LANE_BITS, LOW_BITS, SPLIT_BITS = 7, 11, 6
ROWS, LANES = 16, 128
MEIOSES = LOW_BITS + 2 * SPLIT_BITS
MID, HIGH = LOW_BITS, LOW_BITS + SPLIT_BITS
F32, BF16 = jnp.float32, jnp.bfloat16


def theta_list(theta_ref, marker):
    return [
        BASE_THETA * lax.shift_left(jnp.int32(1), theta_ref[marker, b]).astype(F32)
        for b in range(MEIOSES)
    ]


def anchor_list(mask_ref, marker):
    pairs = []
    for b in range(MEIOSES):
        mask = mask_ref[marker, b]
        zero = jnp.where(mask % 2 == 1, F32(1.0), F32(PENALTY))
        one = jnp.where(mask // 2 == 1, F32(1.0), F32(PENALTY))
        pairs.append((zero, one))
    return pairs


def kron_rows(thetas):
    row = lax.broadcasted_iota(jnp.int32, (8, LANES), 0)
    lane = lax.broadcasted_iota(jnp.int32, (8, LANES), 1)
    low = jnp.ones((8, LANES), F32)
    for b in range(3):
        low = low * jnp.where(((row ^ lane) >> b) & 1 == 1, thetas[b], 1.0 - thetas[b])
    pieces = [low]
    for b in range(3, 7):
        bit = (lane >> b) & 1 == 1
        same = jnp.where(bit, thetas[b], 1.0 - thetas[b])
        other = jnp.where(bit, 1.0 - thetas[b], thetas[b])
        pieces = [p * same for p in pieces] + [p * other for p in pieces]
    return jnp.concatenate(pieces, axis=0)


def two_parts(x):
    high = x.astype(BF16)
    return high, (x - high.astype(F32)).astype(BF16)


def mix_lanes(x, kron):
    high, low = two_parts(x)
    left = jnp.concatenate([high, low, high, low], axis=1)
    right = jnp.concatenate([kron[0], kron[0], kron[1], kron[1]], axis=0)
    return jnp.dot(left, right, preferred_element_type=F32)


def mix_row_bits(kron, x):
    high, low = two_parts(x)
    left = jnp.concatenate([kron[0], kron[0], kron[1], kron[1]], axis=1)
    right = jnp.concatenate([high, low, high, low], axis=0)
    return jnp.dot(left, right, preferred_element_type=F32)


def mix_blocks(chunks, lanes, rows):
    mixed = mix_lanes(jnp.concatenate(chunks, axis=0), lanes)
    mixed = mix_row_bits(rows, jnp.concatenate([mixed[:128], mixed[128:]], axis=1))
    return [
        mixed[j * ROWS : (j + 1) * ROWS, half * LANES : (half + 1) * LANES]
        for half in range(2)
        for j in range(8)
    ]


def butterfly(values, thetas):
    values = list(values)
    for b, theta in enumerate(thetas):
        step = 1 << b
        for i in range(len(values)):
            if i & step == 0:
                moved = theta * (values[i + step] - values[i])
                values[i], values[i + step] = values[i] + moved, values[i + step] - moved
    return values


def low_factor(anchors):
    row = lax.broadcasted_iota(jnp.int32, (ROWS, LANES), 0)
    lane = lax.broadcasted_iota(jnp.int32, (ROWS, LANES), 1)
    position = row * LANES + lane
    result = jnp.full((ROWS, LANES), 1.0 - ERROR_RATE, F32)
    for b in range(LOW_BITS):
        zero, one = anchors[b]
        result = result * jnp.where((position >> b) & 1 == 1, one, zero)
    return result


def device_factor(anchors, first, device):
    result = F32(1.0)
    for b in range(SPLIT_BITS):
        zero, one = anchors[first + b]
        result = result * jnp.where((device >> b) & 1 == 1, one, zero)
    return result


def three_bits(anchors, first):
    factors = [None] * 8
    for i in range(8):
        value = anchors[first][i & 1]
        for b in (1, 2):
            value = value * anchors[first + b][(i >> b) & 1]
        factors[i] = value
    return factors


def low_table(anchors, first_device, device):
    return low_factor(anchors) * device_factor(anchors, first_device, device)


THETAS, FACTORS, TABLE = 0, 64, 128


def table_thetas(table_ref, marker):
    return [table_ref[THETAS + 32 * marker + b] for b in range(MEIOSES)]


def emitted(table_ref, low_ref, layout, i, j):
    scalar = table_ref[FACTORS + 16 * layout + i] * table_ref[FACTORS + 16 * layout + 8 + j]
    return ERROR_RATE + scalar * low_ref[layout]


def first_kernel(theta_ref, mask_ref, device_ref, fwd_ref, bwd_ref, out_ref, table_ref, low_ref, kron_ref, rows_ref,
                 fwd_in, bwd_in, tmp, sems):
    copies = [
        [
            pltpu.make_async_copy(
                source.at[pl.ds(p * 256, 256), :], target.at[pl.ds(p * 256, 256), :], sems.at[which, p]
            )
            for p in range(4)
        ]
        for which, (source, target) in enumerate(((fwd_ref, fwd_in), (bwd_ref, bwd_in)))
    ]
    for row in copies:
        for copy in row:
            copy.start()
    device = device_ref[0]
    thetas = [theta_list(theta_ref, m) for m in range(2)]
    for m in range(2):
        for b in range(MEIOSES):
            table_ref[THETAS + 32 * m + b] = thetas[m][b]
    for layout, (marker, chunk, own) in enumerate(((0, HIGH, MID), (1, MID, HIGH))):
        anchors = anchor_list(mask_ref, marker)
        low_ref[layout] = low_table(anchors, own, device)
        for at, bits in ((0, chunk + 3), (8, chunk)):
            for i, value in enumerate(three_bits(anchors, bits)):
                table_ref[FACTORS + 16 * layout + at + i] = value
    for m in range(2):
        for part, value in enumerate(two_parts(kron_rows(thetas[m][:7]))):
            kron_ref[m, part] = value
        for part, value in enumerate(two_parts(kron_rows(thetas[m][7:14]))):
            rows_ref[m, part] = value
    for part, value in enumerate(two_parts(kron_rows(thetas[1][7:11] + thetas[1][17:20]))):
        rows_ref[2, part] = value
    for which, source in enumerate((fwd_in, bwd_in)):
        for p in range(4):
            copies[which][p].wait()
            chunks = [source[pl.ds(p * 256 + k * ROWS, ROWS), :] for k in range(16)]
            if which == 1:
                chunks = [
                    chunks[k] * emitted(table_ref, low_ref, 1, 2 * p + k // 8, k % 8)
                    for k in range(16)
                ]
            chunks = mix_blocks(chunks, kron_ref[which], rows_ref[which])
            for k in range(16):
                tmp[which, 16 * p + k] = chunks[k]
        for j in range(8):
            chunks = butterfly([tmp[which, 8 * i + j] for i in range(8)], thetas[which][14:17])
            for i in range(8):
                out_ref[8 * i + j, pl.ds(which * ROWS, ROWS), :] = chunks[i]


def second_kernel(table_ref, in_ref, low_ref, kron_ref, rows_ref, out_ref, tmp):
    thetas = [table_thetas(table_ref, m) for m in range(2)]
    for which in range(2):
        before, after = thetas[which], thetas[1 - which]
        rows = pl.ds(which * ROWS, ROWS)
        for j in range(8):
            chunks = butterfly([in_ref[8 * i + j, rows, :] for i in range(8)], before[20:23])
            for i in range(8):
                tmp[which, 8 * i + j] = chunks[i]
        for pair in range(4):
            both = []
            for i in (2 * pair, 2 * pair + 1):
                chunks = butterfly([tmp[which, 8 * i + j] for j in range(8)], before[17:20])
                chunks = [chunks[j] * emitted(table_ref, low_ref, 0, i, j) for j in range(8)]
                if which == 1:
                    chunks = butterfly(chunks, after[17:20])
                both += chunks
            if which == 0:
                both = mix_blocks(both, kron_ref[1], rows_ref[2])
            for k in range(16):
                tmp[which, 16 * pair + k] = both[k]
        for j in range(8):
            chunks = butterfly([tmp[which, 8 * i + j] for i in range(8)], after[20:23])
            for i in range(8):
                out_ref[8 * i + j, rows, :] = chunks[i]


def forward_kernel(table_ref, in_ref, low_ref, out_ref, sum_ref, tmp):
    thetas = table_thetas(table_ref, 1)
    for i in range(8):
        chunks = butterfly([in_ref[8 * i + j, pl.ds(0, ROWS), :] for j in range(8)], thetas[11:14])
        for j in range(8):
            tmp[8 * i + j] = chunks[j]
    acc = jnp.zeros((ROWS, LANES), F32)
    for j in range(8):
        chunks = butterfly([tmp[8 * i + j] for i in range(8)], thetas[14:17])
        for i in range(8):
            value = chunks[i] * emitted(table_ref, low_ref, 1, i, j)
            acc = acc + value
            out_ref[pl.ds((8 * i + j) * ROWS, ROWS), :] = value
    sum_ref[...] = acc[:8] + acc[8:]


def backward_kernel(table_ref, in_ref, kron_ref, rows_ref, out_ref, sum_ref, tmp):
    thetas = table_thetas(table_ref, 0)
    for p in range(4):
        chunks = [in_ref[16 * p + k, pl.ds(ROWS, ROWS), :] for k in range(16)]
        chunks = mix_blocks(chunks, kron_ref[0], rows_ref[0])
        for k in range(16):
            tmp[16 * p + k] = chunks[k]
    acc = jnp.zeros((ROWS, LANES), F32)
    for j in range(8):
        chunks = butterfly([tmp[8 * i + j] for i in range(8)], thetas[14:17])
        for i in range(8):
            acc = acc + chunks[i]
            out_ref[pl.ds((8 * i + j) * ROWS, ROWS), :] = chunks[i]
    sum_ref[...] = acc[:8] + acc[8:]


def product_kernel(seg_ref, got_ref, bwd_ref, fsum_ref, bsum_ref, first_ref, out_ref, sum_ref, first_in, sem):
    is_first = seg_ref[0] == 0

    @pl.when(is_first)
    def _():
        copy = pltpu.make_async_copy(first_ref, first_in, sem)
        copy.start()
        copy.wait()

    def multiply(left_ref):
        acc = jnp.zeros((8, LANES), F32)
        for i in range(16):
            rows = pl.ds(64 * i, 64)
            value = left_ref[rows, :] * bwd_ref[rows, :]
            out_ref[rows, :] = value
            acc = acc + jnp.sum(value.reshape(8, 8, LANES), axis=0)
        lane = lax.broadcasted_iota(jnp.int32, (1, LANES), 1)
        row = jnp.where(
            lane == 0,
            jnp.sum(fsum_ref[...]),
            jnp.where(lane == 1, jnp.sum(bsum_ref[...]), jnp.sum(acc)),
        )
        sum_ref[...] = jnp.broadcast_to(row[None], sum_ref.shape)

    pl.when(is_first)(lambda: multiply(first_in))
    pl.when(jnp.logical_not(is_first))(lambda: multiply(got_ref))


def scale_kernel(total_ref, fwd_ref, bwd_ref, post_ref, fwd_out, bwd_out, post_out, log_ref, ready, sems):
    totals = jnp.sum(total_ref[...], axis=0)
    means = totals * (1.0 / 2.0**MEIOSES)
    lane = lax.broadcasted_iota(jnp.int32, (1, LANES), 1)
    copies = []
    for which, (source, target) in enumerate(
        ((fwd_ref, fwd_out), (bwd_ref, bwd_out), (post_ref, post_out))
    ):
        mean = jnp.sum(jnp.where(lane == which, means, 0.0), axis=1, keepdims=True)
        scale = 1.0 / mean
        for half in range(2):
            for i in range(4):
                rows = pl.ds(half * 512 + 128 * i, 128)
                ready[which, rows, :] = source[rows, :] * scale
            rows = pl.ds(half * 512, 512)
            copy = pltpu.make_async_copy(
                ready.at[which, rows, :], target.at[rows, :], sems.at[which, half]
            )
            copy.start()
            copies.append(copy)
        if which < 2:
            log_ref[:, pl.ds(which, 1)] = jnp.log(mean)
    for copy in copies:
        copy.wait()


SMEM = pl.BlockSpec(memory_space=pltpu.SMEM)
VMEM = pl.BlockSpec(memory_space=pltpu.VMEM)
ANY = pl.BlockSpec(memory_space=pl.ANY)


def kept(array):
    return pltpu.with_memory_space_constraint(array, pltpu.VMEM)


def vmem(*shape, dtype=F32):
    return (VMEM, pltpu.VMEM(shape, dtype))


def exchanged(blocks):
    return lax.all_to_all(blocks, "state", split_axis=0, concat_axis=0, tiled=True)


def call(kernel, name, scalars, vectors, raw, outs, scratch=()):
    return pl.pallas_call(
        kernel,
        name=name,
        in_specs=[SMEM] * len(scalars) + [VMEM] * len(vectors) + [ANY] * len(raw),
        out_specs=[o[0] for o in outs],
        out_shape=[o[1] for o in outs],
        scratch_shapes=scratch,
    )(*scalars, *[kept(v) for v in vectors], *raw)


def shards(forward_in, backward_in, compat_masks, theta_index):
    groups = lax.axis_size("state")
    pair = (groups, 2 * ROWS, LANES)
    flat = (groups * ROWS, LANES)
    chunk = (groups, ROWS, LANES)
    device = lax.axis_index("state").reshape(1)
    seg = lax.axis_index("seg").reshape(1)
    first = forward_in.reshape(flat)
    both, table, low, kron, rows = call(
        first_kernel,
        "first",
        (theta_index, compat_masks, device),
        (),
        (first, backward_in.reshape(flat)),
        [
            vmem(*pair),
            (SMEM, jax.ShapeDtypeStruct((TABLE,), F32)),
            vmem(2, ROWS, LANES),
            vmem(2, 2, LANES, LANES, dtype=BF16),
            vmem(3, 2, LANES, LANES, dtype=BF16),
        ],
        [
            pltpu.VMEM(flat, F32),
            pltpu.VMEM(flat, F32),
            pltpu.VMEM((2, *chunk), F32),
            pltpu.SemaphoreType.DMA((2, 4)),
        ],
    )
    both = exchanged(both)
    (both,) = call(
        second_kernel,
        "second",
        (table,),
        (both, low, kron, rows),
        (),
        [vmem(*pair)],
        [pltpu.VMEM((2, *chunk), F32)],
    )
    both = exchanged(both)
    forward, fsum = call(
        forward_kernel,
        "forward",
        (table,),
        (both, low),
        (),
        [vmem(*flat), vmem(8, LANES)],
        [pltpu.VMEM(chunk, F32)],
    )
    count = lax.axis_size("seg")
    received = lax.ppermute(forward, "seg", [(s, s + 1) for s in range(count - 1)])
    backward, bsum = call(
        backward_kernel,
        "backward",
        (table,),
        (both, kron, rows),
        (),
        [vmem(*flat), vmem(8, LANES)],
        [pltpu.VMEM(chunk, F32)],
    )
    product, sums = call(
        product_kernel,
        "product",
        (seg,),
        (received, backward, fsum, bsum),
        (first,),
        [vmem(*flat), vmem(groups, 1, LANES)],
        [pltpu.VMEM(flat, F32), pltpu.SemaphoreType.DMA(())],
    )
    whole = (ANY, jax.ShapeDtypeStruct(flat, F32))
    forward, backward, posterior, logs = call(
        scale_kernel,
        "scale",
        (),
        (exchanged(sums), forward, backward, product),
        (),
        [whole, whole, whole, (VMEM, jax.ShapeDtypeStruct((1, 2), F32))],
        [pltpu.VMEM((3, *flat), F32), pltpu.SemaphoreType.DMA((3, 2))],
    )
    return (
        forward.reshape(1, -1),
        backward.reshape(1, -1),
        posterior.reshape(1, -1),
        logs.reshape(2, 1),
    )


def solution(mesh):
    placed = (P("seg", "state"), P("seg", "state"), P("seg", None), P("seg", None))
    return jax.shard_map(
        shards,
        mesh=mesh,
        in_specs=placed,
        out_specs=(P("seg", "state"), P("seg", "state"), P("seg", "state"), P(None, "seg")),
        check_vma=False,
    )
```

```python
import jax
import jax.numpy as jnp
from jax import lax
from jax.experimental import pallas as pl
from jax.experimental.pallas import tpu as pltpu
from jax.sharding import PartitionSpec as P

PENALTY = 0.5
ERROR_RATE = 0.02
BASE_THETA = 0.01
LANE_BITS, LOW_BITS, SPLIT_BITS = 7, 11, 6
ROWS, LANES = 16, 128
MEIOSES = LOW_BITS + 2 * SPLIT_BITS
MID, HIGH = LOW_BITS, LOW_BITS + SPLIT_BITS
F32, BF16 = jnp.float32, jnp.bfloat16


def theta_list(theta_ref, marker):
    return [
        BASE_THETA * lax.shift_left(jnp.int32(1), theta_ref[marker, b]).astype(F32)
        for b in range(MEIOSES)
    ]


def anchor_list(mask_ref, marker):
    pairs = []
    for b in range(MEIOSES):
        mask = mask_ref[marker, b]
        zero = jnp.where(mask & 1 == 1, F32(1.0), F32(PENALTY))
        one = jnp.where(mask >> 1 == 1, F32(1.0), F32(PENALTY))
        pairs.append((zero, one))
    return pairs


def kron_rows(thetas):
    row = lax.broadcasted_iota(jnp.int32, (8, LANES), 0)
    lane = lax.broadcasted_iota(jnp.int32, (8, LANES), 1)
    low = jnp.ones((8, LANES), F32)
    for b in range(3):
        low = low * jnp.where(((row ^ lane) >> b) & 1 == 1, thetas[b], 1.0 - thetas[b])
    pieces = [low]
    for b in range(3, 7):
        bit = (lane >> b) & 1 == 1
        same = jnp.where(bit, thetas[b], 1.0 - thetas[b])
        other = jnp.where(bit, 1.0 - thetas[b], thetas[b])
        pieces = [p * same for p in pieces] + [p * other for p in pieces]
    return jnp.concatenate(pieces, axis=0)


def two_parts(x):
    high = x.astype(BF16)
    return high, (x - high.astype(F32)).astype(BF16)


def mix_lanes(x, kron):
    high, low = two_parts(x)
    left = jnp.concatenate([high, low, high, low], axis=1)
    right = jnp.concatenate([kron[0], kron[0], kron[1], kron[1]], axis=0)
    return jnp.dot(left, right, preferred_element_type=F32)


def mix_row_bits(kron, x):
    high, low = two_parts(x)
    left = jnp.concatenate([kron[0], kron[0], kron[1], kron[1]], axis=1)
    right = jnp.concatenate([high, low, high, low], axis=0)
    return jnp.dot(left, right, preferred_element_type=F32)


def mix_blocks(chunks, lanes, rows):
    count = len(chunks) // 8
    mixed = mix_lanes(jnp.concatenate(chunks, axis=0), lanes)
    side_by_side = jnp.concatenate([mixed[i * 128 : (i + 1) * 128] for i in range(count)], axis=1)
    mixed = mix_row_bits(rows, side_by_side)
    return [
        mixed[j * ROWS : (j + 1) * ROWS, i * LANES : (i + 1) * LANES]
        for i in range(count)
        for j in range(8)
    ]


def butterfly(values, thetas):
    values = list(values)
    for b, theta in enumerate(thetas):
        step = 1 << b
        for i in range(len(values)):
            if i & step == 0:
                moved = theta * (values[i + step] - values[i])
                values[i], values[i + step] = values[i] + moved, values[i + step] - moved
    return values


def low_factor(anchors):
    row = lax.broadcasted_iota(jnp.int32, (ROWS, LANES), 0)
    lane = lax.broadcasted_iota(jnp.int32, (ROWS, LANES), 1)
    position = row * LANES + lane
    result = jnp.full((ROWS, LANES), 1.0 - ERROR_RATE, F32)
    for b in range(LOW_BITS):
        zero, one = anchors[b]
        result = result * jnp.where((position >> b) & 1 == 1, one, zero)
    return result


def device_factor(anchors, first, device):
    result = F32(1.0)
    for b in range(SPLIT_BITS):
        zero, one = anchors[first + b]
        result = result * jnp.where((device >> b) & 1 == 1, one, zero)
    return result


def three_bits(anchors, first):
    factors = [None] * 8
    for i in range(8):
        value = anchors[first][i & 1]
        for b in (1, 2):
            value = value * anchors[first + b][(i >> b) & 1]
        factors[i] = value
    return factors


def low_table(anchors, first_device, device):
    return low_factor(anchors) * device_factor(anchors, first_device, device)


THETAS, FACTORS, TABLE = 0, 64, 96
PARTS = 1


def table_thetas(table_ref, marker):
    return [table_ref[pl.ds(THETAS + 32 * marker + b, 1), :] for b in range(MEIOSES)]


def emitted(table_ref, low_ref, layout, i, j):
    outer = table_ref[pl.ds(FACTORS + 16 * layout + i, 1), :]
    inner = table_ref[pl.ds(FACTORS + 16 * layout + 8 + j, 1), :]
    return ERROR_RATE + (outer * inner) * low_ref[layout]


def first_kernel(theta_hbm, mask_hbm, fwd_ref, bwd_ref, out_ref, table_ref, low_ref, kron_ref, rows_ref,
                 theta_ref, mask_ref, fwd_in, bwd_in, tmp, small, sems):
    scalars = [
        pltpu.make_async_copy(source, target, small.at[k])
        for k, (source, target) in enumerate(((theta_hbm, theta_ref), (mask_hbm, mask_ref)))
    ]
    for copy in scalars:
        copy.start()
    copies = [
        [
            pltpu.make_async_copy(
                source.at[pl.ds(p * 256, 256), :], target.at[pl.ds(p * 256, 256), :], sems.at[which, p]
            )
            for p in range(4)
        ]
        for which, (source, target) in enumerate(((fwd_ref, fwd_in), (bwd_ref, bwd_in)))
    ]
    for row in copies:
        for copy in row:
            copy.start()
    device = lax.axis_index("state")
    for copy in scalars:
        copy.wait()
    thetas = [theta_list(theta_ref, m) for m in range(2)]
    for m in range(2):
        for b in range(MEIOSES):
            table_ref[pl.ds(THETAS + 32 * m + b, 1), :] = jnp.full((1, LANES), thetas[m][b], F32)
    for layout, (marker, chunk, own) in enumerate(((0, HIGH, MID), (1, MID, HIGH))):
        anchors = anchor_list(mask_ref, marker)
        low_ref[layout] = low_table(anchors, own, device)
        for at, bits in ((0, chunk + 3), (8, chunk)):
            for i, value in enumerate(three_bits(anchors, bits)):
                table_ref[pl.ds(FACTORS + 16 * layout + at + i, 1), :] = jnp.full((1, LANES), value, F32)
    for m in range(2):
        for part, value in enumerate(two_parts(kron_rows(thetas[m][:7]))):
            kron_ref[m, part] = value
        for part, value in enumerate(two_parts(kron_rows(thetas[m][7:14]))):
            rows_ref[m, part] = value
    for part, value in enumerate(two_parts(kron_rows(thetas[1][7:11] + thetas[1][17:20]))):
        rows_ref[2, part] = value
    for which, source in enumerate((fwd_in, bwd_in)):
        for copy in copies[which]:
            copy.wait()
        for p in range(PARTS):
            first = p * 64 // PARTS
            chunks = [source[pl.ds((first + k) * ROWS, ROWS), :] for k in range(64 // PARTS)]
            if which == 1:
                chunks = [
                    chunk * emitted(table_ref, low_ref, 1, (first + k) // 8, k % 8)
                    for k, chunk in enumerate(chunks)
                ]
            chunks = mix_blocks(chunks, kron_ref[which], rows_ref[which])
            for k, chunk in enumerate(chunks):
                tmp[which, first + k] = chunk
        for j in range(8):
            chunks = butterfly([tmp[which, 8 * i + j] for i in range(8)], thetas[which][14:17])
            for i in range(8):
                out_ref[8 * i + j, pl.ds(which * ROWS, ROWS), :] = chunks[i]


def second_kernel(table_ref, in_ref, low_ref, kron_ref, rows_ref, out_ref, tmp):
    thetas = [table_thetas(table_ref, m) for m in range(2)]
    for which in range(2):
        before, after = thetas[which], thetas[1 - which]
        rows = pl.ds(which * ROWS, ROWS)
        for j in range(8):
            chunks = butterfly([in_ref[8 * i + j, rows, :] for i in range(8)], before[20:23])
            for i in range(8):
                tmp[which, 8 * i + j] = chunks[i]
        for p in range(PARTS):
            first = p * 64 // PARTS
            both = []
            for i in range(first // 8, (first + 64 // PARTS) // 8):
                chunks = butterfly([tmp[which, 8 * i + j] for j in range(8)], before[17:20])
                chunks = [chunks[j] * emitted(table_ref, low_ref, 0, i, j) for j in range(8)]
                if which == 1:
                    chunks = butterfly(chunks, after[17:20])
                both += chunks
            if which == 0:
                both = mix_blocks(both, kron_ref[1], rows_ref[2])
            for k, chunk in enumerate(both):
                tmp[which, first + k] = chunk
        for j in range(8):
            chunks = butterfly([tmp[which, 8 * i + j] for i in range(8)], after[20:23])
            for i in range(8):
                out_ref[8 * i + j, rows, :] = chunks[i]


def forward_kernel(table_ref, in_ref, low_ref, out_ref, sum_ref, tmp):
    thetas = table_thetas(table_ref, 1)
    for i in range(8):
        chunks = butterfly([in_ref[8 * i + j, pl.ds(0, ROWS), :] for j in range(8)], thetas[11:14])
        for j in range(8):
            tmp[8 * i + j] = chunks[j]
    acc = jnp.zeros((ROWS, LANES), F32)
    for j in range(8):
        chunks = butterfly([tmp[8 * i + j] for i in range(8)], thetas[14:17])
        for i in range(8):
            value = chunks[i] * emitted(table_ref, low_ref, 1, i, j)
            acc = acc + value
            out_ref[pl.ds((8 * i + j) * ROWS, ROWS), :] = value
    sum_ref[...] = acc[:8] + acc[8:]


def backward_kernel(table_ref, in_ref, kron_ref, rows_ref, out_ref, sum_ref, tmp):
    thetas = table_thetas(table_ref, 0)
    for p in range(PARTS):
        first = p * 64 // PARTS
        chunks = [in_ref[first + k, pl.ds(ROWS, ROWS), :] for k in range(64 // PARTS)]
        for k, chunk in enumerate(mix_blocks(chunks, kron_ref[0], rows_ref[0])):
            tmp[first + k] = chunk
    acc = jnp.zeros((ROWS, LANES), F32)
    for j in range(8):
        chunks = butterfly([tmp[8 * i + j] for i in range(8)], thetas[14:17])
        for i in range(8):
            acc = acc + chunks[i]
            out_ref[pl.ds((8 * i + j) * ROWS, ROWS), :] = chunks[i]
    sum_ref[...] = acc[:8] + acc[8:]


def product_kernel(got_ref, bwd_ref, fsum_ref, bsum_ref, first_ref, _, out_ref, sum_ref, first_in, sem):
    is_first = lax.axis_index("seg") == 0

    @pl.when(is_first)
    def _():
        copy = pltpu.make_async_copy(first_ref, first_in, sem)
        copy.start()
        copy.wait()

    def multiply(left_ref):
        acc = jnp.zeros((8, LANES), F32)
        for i in range(16):
            rows = pl.ds(64 * i, 64)
            value = left_ref[rows, :] * bwd_ref[rows, :]
            out_ref[rows, :] = value
            acc = acc + jnp.sum(value.reshape(8, 8, LANES), axis=0)
        lane = lax.broadcasted_iota(jnp.int32, (1, LANES), 1)
        row = jnp.where(
            lane == 0,
            jnp.sum(fsum_ref[...]),
            jnp.where(lane == 1, jnp.sum(bsum_ref[...]), jnp.sum(acc)),
        )
        sum_ref[...] = jnp.broadcast_to(row[None], sum_ref.shape)

    pl.when(is_first)(lambda: multiply(first_in))
    pl.when(jnp.logical_not(is_first))(lambda: multiply(got_ref))


def scale_kernel(total_ref, fwd_ref, bwd_ref, post_ref, fwd_out, bwd_out, post_out, log_ref, ready, sems):
    totals = jnp.sum(total_ref[...], axis=0)
    means = totals * (1.0 / 2.0**MEIOSES)
    lane = lax.broadcasted_iota(jnp.int32, (1, LANES), 1)
    copies = []
    for which, (source, target) in enumerate(
        ((fwd_ref, fwd_out), (bwd_ref, bwd_out), (post_ref, post_out))
    ):
        mean = jnp.sum(jnp.where(lane == which, means, 0.0), axis=1, keepdims=True)
        scale = 1.0 / mean
        for half in range(2):
            for i in range(4):
                rows = pl.ds(half * 512 + 128 * i, 128)
                ready[which, rows, :] = source[rows, :] * scale
            rows = pl.ds(half * 512, 512)
            copy = pltpu.make_async_copy(
                ready.at[which, rows, :], target.at[rows, :], sems.at[which, half]
            )
            copy.start()
            copies.append(copy)
        if which < 2:
            log_ref[:, pl.ds(which, 1)] = jnp.log(mean)
    for copy in copies:
        copy.wait()


VMEM = pl.BlockSpec(memory_space=pltpu.VMEM)
ANY = pl.BlockSpec(memory_space=pl.ANY)


def kept(array):
    return pltpu.with_memory_space_constraint(array, pltpu.VMEM)


def vmem(*shape, dtype=F32):
    return (VMEM, pltpu.VMEM(shape, dtype))


def exchanged(blocks):
    return lax.all_to_all(blocks, "state", split_axis=0, concat_axis=0, tiled=True)


def call(kernel, name, vectors, raw, outs, scratch=()):
    return pl.pallas_call(
        kernel,
        name=name,
        in_specs=[VMEM] * len(vectors) + [ANY] * len(raw),
        out_specs=[o[0] for o in outs],
        out_shape=[o[1] for o in outs],
        scratch_shapes=scratch,
    )(*[kept(v) for v in vectors], *raw)


def shards(forward_in, backward_in, compat_masks, theta_index):
    groups = lax.axis_size("state")
    pair = (groups, 2 * ROWS, LANES)
    flat = (groups * ROWS, LANES)
    chunk = (groups, ROWS, LANES)
    first = forward_in.reshape(flat)
    both, table, low, kron, rows = call(
        first_kernel,
        "first",
        (),
        (theta_index, compat_masks, first, backward_in.reshape(flat)),
        [
            vmem(*pair),
            vmem(TABLE, LANES),
            vmem(2, ROWS, LANES),
            vmem(2, 2, LANES, LANES, dtype=BF16),
            vmem(3, 2, LANES, LANES, dtype=BF16),
        ],
        [
            pltpu.SMEM(theta_index.shape, jnp.int32),
            pltpu.SMEM(compat_masks.shape, jnp.int32),
            pltpu.VMEM(flat, F32),
            pltpu.VMEM(flat, F32),
            pltpu.VMEM((2, *chunk), F32),
            pltpu.SemaphoreType.DMA((2,)),
            pltpu.SemaphoreType.DMA((2, 4)),
        ],
    )
    both = exchanged(both)
    (both,) = call(
        second_kernel,
        "second",
        (table, both, low, kron, rows),
        (),
        [vmem(*pair)],
        [pltpu.VMEM((2, *chunk), F32)],
    )
    both = exchanged(both)
    forward, fsum = call(
        forward_kernel,
        "forward",
        (table, both, low),
        (),
        [vmem(*flat), vmem(8, LANES)],
        [pltpu.VMEM(chunk, F32)],
    )
    count = lax.axis_size("seg")
    received = lax.ppermute(forward, "seg", [(s, s + 1) for s in range(count - 1)])
    backward, bsum = call(
        backward_kernel,
        "backward",
        (table, both, kron, rows),
        (),
        [vmem(*flat), vmem(8, LANES)],
        [pltpu.VMEM(chunk, F32)],
    )
    product, sums = call(
        product_kernel,
        "product",
        (received, backward, fsum, bsum),
        (first, lax.axis_index("seg").reshape(1)),
        [vmem(*flat), vmem(groups, 1, LANES)],
        [pltpu.VMEM(flat, F32), pltpu.SemaphoreType.DMA(())],
    )
    whole = (ANY, jax.ShapeDtypeStruct(flat, F32))
    forward, backward, posterior, logs = call(
        scale_kernel,
        "scale",
        (exchanged(sums), forward, backward, product),
        (),
        [whole, whole, whole, (VMEM, jax.ShapeDtypeStruct((1, 2), F32))],
        [pltpu.VMEM((3, *flat), F32), pltpu.SemaphoreType.DMA((3, 2))],
    )
    return (
        forward.reshape(1, -1),
        backward.reshape(1, -1),
        posterior.reshape(1, -1),
        logs.reshape(2, 1),
    )


def solution(mesh):
    placed = (P("seg", "state"), P("seg", "state"), P("seg", None), P("seg", None))
    return jax.shard_map(
        shards,
        mesh=mesh,
        in_specs=placed,
        out_specs=(P("seg", "state"), P("seg", "state"), P("seg", "state"), P(None, "seg")),
        check_vma=False,
    )
```

```python
import jax
import jax.numpy as jnp
from jax import lax
from jax.experimental import pallas as pl
from jax.experimental.pallas import tpu as pltpu
from jax.sharding import PartitionSpec as P

PENALTY = 0.5
ERROR_RATE = 0.02
BASE_THETA = 0.01
LANE_BITS, LOW_BITS, SPLIT_BITS = 7, 11, 6
ROWS, LANES = 16, 128
MEIOSES = LOW_BITS + 2 * SPLIT_BITS
MID, HIGH = LOW_BITS, LOW_BITS + SPLIT_BITS
F32, BF16 = jnp.float32, jnp.bfloat16


def theta_list(theta_ref, marker):
    return [
        BASE_THETA * lax.shift_left(jnp.int32(1), theta_ref[marker, b]).astype(F32)
        for b in range(MEIOSES)
    ]


def anchor_list(mask_ref, marker):
    pairs = []
    for b in range(MEIOSES):
        mask = mask_ref[marker, b]
        zero = jnp.where(mask & 1 == 1, F32(1.0), F32(PENALTY))
        one = jnp.where(mask >> 1 == 1, F32(1.0), F32(PENALTY))
        pairs.append((zero, one))
    return pairs


def kron_rows(thetas):
    row = lax.broadcasted_iota(jnp.int32, (8, LANES), 0)
    lane = lax.broadcasted_iota(jnp.int32, (8, LANES), 1)
    low = jnp.ones((8, LANES), F32)
    for b in range(3):
        low = low * jnp.where(((row ^ lane) >> b) & 1 == 1, thetas[b], 1.0 - thetas[b])
    pieces = [low]
    for b in range(3, 7):
        bit = (lane >> b) & 1 == 1
        same = jnp.where(bit, thetas[b], 1.0 - thetas[b])
        other = jnp.where(bit, 1.0 - thetas[b], thetas[b])
        pieces = [p * same for p in pieces] + [p * other for p in pieces]
    return jnp.concatenate(pieces, axis=0)


def two_parts(x):
    high = x.astype(BF16)
    return high, (x - high.astype(F32)).astype(BF16)


def mix_lanes(x, kron):
    left = jnp.concatenate(two_parts(x), axis=1)
    once = jnp.concatenate([kron[0], kron[1]], axis=1)
    both = jnp.dot(left, jnp.concatenate([once, once], axis=0), preferred_element_type=F32)
    return both[:, :LANES] + both[:, LANES:]


def mix_row_bits(kron, x):
    right = jnp.concatenate(two_parts(x), axis=0)
    once = jnp.concatenate([kron[0], kron[1]], axis=0)
    both = jnp.dot(jnp.concatenate([once, once], axis=1), right, preferred_element_type=F32)
    return both[:128] + both[128:]


def mix_blocks(chunks, lanes, rows):
    count = len(chunks) // 8
    mixed = mix_lanes(jnp.concatenate(chunks, axis=0), lanes)
    side_by_side = jnp.concatenate([mixed[i * 128 : (i + 1) * 128] for i in range(count)], axis=1)
    mixed = mix_row_bits(rows, side_by_side)
    return [
        mixed[j * ROWS : (j + 1) * ROWS, i * LANES : (i + 1) * LANES]
        for i in range(count)
        for j in range(8)
    ]


def butterfly(values, thetas):
    values = list(values)
    for b, theta in enumerate(thetas):
        step = 1 << b
        for i in range(len(values)):
            if i & step == 0:
                moved = theta * (values[i + step] - values[i])
                values[i], values[i + step] = values[i] + moved, values[i + step] - moved
    return values


def low_factor(anchors):
    row = lax.broadcasted_iota(jnp.int32, (ROWS, LANES), 0)
    lane = lax.broadcasted_iota(jnp.int32, (ROWS, LANES), 1)
    position = row * LANES + lane
    result = jnp.full((ROWS, LANES), 1.0 - ERROR_RATE, F32)
    for b in range(LOW_BITS):
        zero, one = anchors[b]
        result = result * jnp.where((position >> b) & 1 == 1, one, zero)
    return result


def device_factor(anchors, first, device):
    result = F32(1.0)
    for b in range(SPLIT_BITS):
        zero, one = anchors[first + b]
        result = result * jnp.where((device >> b) & 1 == 1, one, zero)
    return result


def three_bits(anchors, first):
    factors = [None] * 8
    for i in range(8):
        value = anchors[first][i & 1]
        for b in (1, 2):
            value = value * anchors[first + b][(i >> b) & 1]
        factors[i] = value
    return factors


def low_table(anchors, first_device, device):
    return low_factor(anchors) * device_factor(anchors, first_device, device)


THETAS, FACTORS, TABLE = 0, 64, 96
PARTS = 1


def table_thetas(table_ref, marker):
    return [table_ref[pl.ds(THETAS + 32 * marker + b, 1), :] for b in range(MEIOSES)]


def emitted(table_ref, low_ref, layout, i, j):
    outer = table_ref[pl.ds(FACTORS + 16 * layout + i, 1), :]
    inner = table_ref[pl.ds(FACTORS + 16 * layout + 8 + j, 1), :]
    return ERROR_RATE + (outer * inner) * low_ref[layout]


def first_kernel(theta_hbm, mask_hbm, fwd_ref, bwd_ref, out_ref, table_ref, low_ref, kron_ref, rows_ref,
                 theta_ref, mask_ref, fwd_in, bwd_in, tmp, small, sems):
    scalars = [
        pltpu.make_async_copy(source, target, small.at[k])
        for k, (source, target) in enumerate(((theta_hbm, theta_ref), (mask_hbm, mask_ref)))
    ]
    for copy in scalars:
        copy.start()
    copies = [
        [pltpu.make_async_copy(source, target, sems.at[which])]
        for which, (source, target) in enumerate(((fwd_ref, fwd_in), (bwd_ref, bwd_in)))
    ]
    for row in copies:
        for copy in row:
            copy.start()
    device = lax.axis_index("state")
    for copy in scalars:
        copy.wait()
    thetas = [theta_list(theta_ref, m) for m in range(2)]
    for m in range(2):
        for b in range(MEIOSES):
            table_ref[pl.ds(THETAS + 32 * m + b, 1), :] = jnp.full((1, LANES), thetas[m][b], F32)
    for layout, (marker, chunk, own) in enumerate(((0, HIGH, MID), (1, MID, HIGH))):
        anchors = anchor_list(mask_ref, marker)
        low_ref[layout] = low_table(anchors, own, device)
        for at, bits in ((0, chunk + 3), (8, chunk)):
            for i, value in enumerate(three_bits(anchors, bits)):
                table_ref[pl.ds(FACTORS + 16 * layout + at + i, 1), :] = jnp.full((1, LANES), value, F32)
    for m in range(2):
        for part, value in enumerate(two_parts(kron_rows(thetas[m][:7]))):
            kron_ref[m, part] = value
        for part, value in enumerate(two_parts(kron_rows(thetas[m][7:14]))):
            rows_ref[m, part] = value
    for part, value in enumerate(two_parts(kron_rows(thetas[1][7:11] + thetas[1][17:20]))):
        rows_ref[2, part] = value
    for row in copies:
        row[0].wait()
    for which, source in enumerate((fwd_in, bwd_in)):
        for p in range(PARTS):
            first = p * 64 // PARTS
            chunks = [source[pl.ds((first + k) * ROWS, ROWS), :] for k in range(64 // PARTS)]
            if which == 1:
                chunks = [
                    chunk * emitted(table_ref, low_ref, 1, (first + k) // 8, k % 8)
                    for k, chunk in enumerate(chunks)
                ]
            chunks = mix_blocks(chunks, kron_ref[which], rows_ref[which])
            for k, chunk in enumerate(chunks):
                tmp[which, first + k] = chunk
        for j in range(8):
            chunks = butterfly([tmp[which, 8 * i + j] for i in range(8)], thetas[which][14:17])
            for i in range(8):
                out_ref[8 * i + j, pl.ds(which * ROWS, ROWS), :] = chunks[i]


def second_kernel(table_ref, in_ref, low_ref, kron_ref, rows_ref, out_ref, tmp):
    thetas = [table_thetas(table_ref, m) for m in range(2)]
    for which in range(2):
        before, after = thetas[which], thetas[1 - which]
        rows = pl.ds(which * ROWS, ROWS)
        for j in range(8):
            chunks = butterfly([in_ref[8 * i + j, rows, :] for i in range(8)], before[20:23])
            for i in range(8):
                tmp[which, 8 * i + j] = chunks[i]
        for p in range(PARTS):
            first = p * 64 // PARTS
            both = []
            for i in range(first // 8, (first + 64 // PARTS) // 8):
                chunks = butterfly([tmp[which, 8 * i + j] for j in range(8)], before[17:20])
                chunks = [chunks[j] * emitted(table_ref, low_ref, 0, i, j) for j in range(8)]
                if which == 1:
                    chunks = butterfly(chunks, after[17:20])
                both += chunks
            if which == 0:
                both = mix_blocks(both, kron_ref[1], rows_ref[2])
            for k, chunk in enumerate(both):
                tmp[which, first + k] = chunk
        for j in range(8):
            chunks = butterfly([tmp[which, 8 * i + j] for i in range(8)], after[20:23])
            for i in range(8):
                out_ref[8 * i + j, rows, :] = chunks[i]


def forward_kernel(table_ref, in_ref, low_ref, out_ref, sum_ref, tmp):
    thetas = table_thetas(table_ref, 1)
    for i in range(8):
        chunks = butterfly([in_ref[8 * i + j, pl.ds(0, ROWS), :] for j in range(8)], thetas[11:14])
        for j in range(8):
            tmp[8 * i + j] = chunks[j]
    acc = jnp.zeros((ROWS, LANES), F32)
    for j in range(8):
        chunks = butterfly([tmp[8 * i + j] for i in range(8)], thetas[14:17])
        for i in range(8):
            value = chunks[i] * emitted(table_ref, low_ref, 1, i, j)
            acc = acc + value
            out_ref[pl.ds((8 * i + j) * ROWS, ROWS), :] = value
    sum_ref[...] = acc[:8] + acc[8:]


def backward_kernel(table_ref, in_ref, kron_ref, rows_ref, out_ref, sum_ref, tmp):
    thetas = table_thetas(table_ref, 0)
    for p in range(PARTS):
        first = p * 64 // PARTS
        chunks = [in_ref[first + k, pl.ds(ROWS, ROWS), :] for k in range(64 // PARTS)]
        for k, chunk in enumerate(mix_blocks(chunks, kron_ref[0], rows_ref[0])):
            tmp[first + k] = chunk
    acc = jnp.zeros((ROWS, LANES), F32)
    for j in range(8):
        chunks = butterfly([tmp[8 * i + j] for i in range(8)], thetas[14:17])
        for i in range(8):
            acc = acc + chunks[i]
            out_ref[pl.ds((8 * i + j) * ROWS, ROWS), :] = chunks[i]
    sum_ref[...] = acc[:8] + acc[8:]


def product_kernel(got_ref, bwd_ref, fsum_ref, bsum_ref, first_ref, _, out_ref, sum_ref, first_in, sem):
    is_first = lax.axis_index("seg") == 0

    @pl.when(is_first)
    def _():
        copy = pltpu.make_async_copy(first_ref, first_in, sem)
        copy.start()
        copy.wait()

    def multiply(left_ref):
        acc = jnp.zeros((8, LANES), F32)
        for i in range(16):
            rows = pl.ds(64 * i, 64)
            value = left_ref[rows, :] * bwd_ref[rows, :]
            out_ref[rows, :] = value
            acc = acc + jnp.sum(value.reshape(8, 8, LANES), axis=0)
        lane = lax.broadcasted_iota(jnp.int32, (1, LANES), 1)
        row = jnp.where(
            lane == 0,
            jnp.sum(fsum_ref[...]),
            jnp.where(lane == 1, jnp.sum(bsum_ref[...]), jnp.sum(acc)),
        )
        sum_ref[...] = jnp.broadcast_to(row[None], sum_ref.shape)

    pl.when(is_first)(lambda: multiply(first_in))
    pl.when(jnp.logical_not(is_first))(lambda: multiply(got_ref))


def scale_kernel(total_ref, fwd_ref, bwd_ref, post_ref, fwd_out, bwd_out, post_out, log_ref, ready, sems):
    totals = jnp.sum(total_ref[...], axis=0)
    means = totals * (1.0 / 2.0**MEIOSES)
    lane = lax.broadcasted_iota(jnp.int32, (1, LANES), 1)
    copies = []
    for which, (source, target) in enumerate(
        ((fwd_ref, fwd_out), (bwd_ref, bwd_out), (post_ref, post_out))
    ):
        mean = jnp.sum(jnp.where(lane == which, means, 0.0), axis=1, keepdims=True)
        scale = 1.0 / mean
        for half in range(2):
            for i in range(4):
                rows = pl.ds(half * 512 + 128 * i, 128)
                ready[which, rows, :] = source[rows, :] * scale
            rows = pl.ds(half * 512, 512)
            copy = pltpu.make_async_copy(
                ready.at[which, rows, :], target.at[rows, :], sems.at[which, half]
            )
            copy.start()
            copies.append(copy)
        if which < 2:
            log_ref[:, pl.ds(which, 1)] = jnp.log(mean)
    for copy in copies:
        copy.wait()


VMEM = pl.BlockSpec(memory_space=pltpu.VMEM)
ANY = pl.BlockSpec(memory_space=pl.ANY)


def kept(array):
    return pltpu.with_memory_space_constraint(array, pltpu.VMEM)


def vmem(*shape, dtype=F32):
    return (VMEM, pltpu.VMEM(shape, dtype))


def exchanged(blocks):
    return lax.all_to_all(blocks, "state", split_axis=0, concat_axis=0, tiled=True)


def call(kernel, name, vectors, raw, outs, scratch=()):
    return pl.pallas_call(
        kernel,
        name=name,
        in_specs=[VMEM] * len(vectors) + [ANY] * len(raw),
        out_specs=[o[0] for o in outs],
        out_shape=[o[1] for o in outs],
        scratch_shapes=scratch,
    )(*[kept(v) for v in vectors], *raw)


def shards(forward_in, backward_in, compat_masks, theta_index):
    groups = lax.axis_size("state")
    pair = (groups, 2 * ROWS, LANES)
    flat = (groups * ROWS, LANES)
    chunk = (groups, ROWS, LANES)
    first = forward_in.reshape(flat)
    both, table, low, kron, rows = call(
        first_kernel,
        "first",
        (),
        (theta_index, compat_masks, first, backward_in.reshape(flat)),
        [
            vmem(*pair),
            vmem(TABLE, LANES),
            vmem(2, ROWS, LANES),
            vmem(2, 2, LANES, LANES, dtype=BF16),
            vmem(3, 2, LANES, LANES, dtype=BF16),
        ],
        [
            pltpu.SMEM(theta_index.shape, jnp.int32),
            pltpu.SMEM(compat_masks.shape, jnp.int32),
            pltpu.VMEM(flat, F32),
            pltpu.VMEM(flat, F32),
            pltpu.VMEM((2, *chunk), F32),
            pltpu.SemaphoreType.DMA((2,)),
            pltpu.SemaphoreType.DMA((2,)),
        ],
    )
    both = exchanged(both)
    (both,) = call(
        second_kernel,
        "second",
        (table, both, low, kron, rows),
        (),
        [vmem(*pair)],
        [pltpu.VMEM((2, *chunk), F32)],
    )
    both = exchanged(both)
    forward, fsum = call(
        forward_kernel,
        "forward",
        (table, both, low),
        (),
        [vmem(*flat), vmem(8, LANES)],
        [pltpu.VMEM(chunk, F32)],
    )
    count = lax.axis_size("seg")
    received = lax.ppermute(forward, "seg", [(s, s + 1) for s in range(count - 1)])
    backward, bsum = call(
        backward_kernel,
        "backward",
        (table, both, kron, rows),
        (),
        [vmem(*flat), vmem(8, LANES)],
        [pltpu.VMEM(chunk, F32)],
    )
    product, sums = call(
        product_kernel,
        "product",
        (received, backward, fsum, bsum),
        (first, lax.axis_index("seg").reshape(1)),
        [vmem(*flat), vmem(groups, 1, LANES)],
        [pltpu.VMEM(flat, F32), pltpu.SemaphoreType.DMA(())],
    )
    whole = (ANY, jax.ShapeDtypeStruct(flat, F32))
    forward, backward, posterior, logs = call(
        scale_kernel,
        "scale",
        (exchanged(sums), forward, backward, product),
        (),
        [whole, whole, whole, (VMEM, jax.ShapeDtypeStruct((1, 2), F32))],
        [pltpu.VMEM((3, *flat), F32), pltpu.SemaphoreType.DMA((3, 2))],
    )
    return (
        forward.reshape(1, -1),
        backward.reshape(1, -1),
        posterior.reshape(1, -1),
        logs.reshape(2, 1),
    )


def solution(mesh):
    placed = (P("seg", "state"), P("seg", "state"), P("seg", None), P("seg", None))
    return jax.shard_map(
        shards,
        mesh=mesh,
        in_specs=placed,
        out_specs=(P("seg", "state"), P("seg", "state"), P("seg", "state"), P(None, "seg")),
        check_vma=False,
    )
```

```python
import jax
import jax.numpy as jnp
from jax import lax
from jax.experimental import pallas as pl
from jax.experimental.pallas import tpu as pltpu
from jax.sharding import PartitionSpec as P

PENALTY = 0.5
ERROR_RATE = 0.02
BASE_THETA = 0.01
LANE_BITS, LOW_BITS, SPLIT_BITS = 7, 11, 6
ROWS, LANES = 16, 128
MEIOSES = LOW_BITS + 2 * SPLIT_BITS
MID, HIGH = LOW_BITS, LOW_BITS + SPLIT_BITS
F32, BF16 = jnp.float32, jnp.bfloat16


def theta_list(theta_ref, marker):
    return [
        BASE_THETA * lax.shift_left(jnp.int32(1), theta_ref[marker, b]).astype(F32)
        for b in range(MEIOSES)
    ]


def anchor_list(mask_ref, marker):
    pairs = []
    for b in range(MEIOSES):
        mask = mask_ref[marker, b]
        zero = jnp.where(mask & 1 == 1, F32(1.0), F32(PENALTY))
        one = jnp.where(mask >> 1 == 1, F32(1.0), F32(PENALTY))
        pairs.append((zero, one))
    return pairs


def kron_rows(thetas):
    row = lax.broadcasted_iota(jnp.int32, (8, LANES), 0)
    lane = lax.broadcasted_iota(jnp.int32, (8, LANES), 1)
    low = jnp.ones((8, LANES), F32)
    for b in range(3):
        low = low * jnp.where(((row ^ lane) >> b) & 1 == 1, thetas[b], 1.0 - thetas[b])
    pieces = [low]
    for b in range(3, 7):
        bit = (lane >> b) & 1 == 1
        same = jnp.where(bit, thetas[b], 1.0 - thetas[b])
        other = jnp.where(bit, 1.0 - thetas[b], thetas[b])
        pieces = [p * same for p in pieces] + [p * other for p in pieces]
    return jnp.concatenate(pieces, axis=0)


def two_parts(x):
    high = x.astype(BF16)
    return high, (x - high.astype(F32)).astype(BF16)


def mix_lanes(x, kron):
    left = jnp.concatenate(two_parts(x), axis=1)
    once = jnp.concatenate([kron[0], kron[1]], axis=1)
    both = jnp.dot(left, jnp.concatenate([once, once], axis=0), preferred_element_type=F32)
    return both[:, :LANES] + both[:, LANES:]


def mix_row_bits(kron, x):
    right = jnp.concatenate(two_parts(x), axis=0)
    once = jnp.concatenate([kron[0], kron[1]], axis=0)
    both = jnp.dot(jnp.concatenate([once, once], axis=1), right, preferred_element_type=F32)
    return both[:128] + both[128:]


def mix_blocks(chunks, lanes, rows):
    count = len(chunks) // 8
    mixed = mix_lanes(jnp.concatenate(chunks, axis=0), lanes)
    side_by_side = jnp.concatenate([mixed[i * 128 : (i + 1) * 128] for i in range(count)], axis=1)
    mixed = mix_row_bits(rows, side_by_side)
    return [
        mixed[j * ROWS : (j + 1) * ROWS, i * LANES : (i + 1) * LANES]
        for i in range(count)
        for j in range(8)
    ]


def butterfly(values, thetas):
    values = list(values)
    for b, theta in enumerate(thetas):
        step = 1 << b
        for i in range(len(values)):
            if i & step == 0:
                moved = theta * (values[i + step] - values[i])
                values[i], values[i + step] = values[i] + moved, values[i + step] - moved
    return values


def low_factor(anchors):
    row = lax.broadcasted_iota(jnp.int32, (ROWS, LANES), 0)
    lane = lax.broadcasted_iota(jnp.int32, (ROWS, LANES), 1)
    position = row * LANES + lane
    result = jnp.full((ROWS, LANES), 1.0 - ERROR_RATE, F32)
    for b in range(LOW_BITS):
        zero, one = anchors[b]
        result = result * jnp.where((position >> b) & 1 == 1, one, zero)
    return result


def device_factor(anchors, first, device):
    result = F32(1.0)
    for b in range(SPLIT_BITS):
        zero, one = anchors[first + b]
        result = result * jnp.where((device >> b) & 1 == 1, one, zero)
    return result


def three_bits(anchors, first):
    factors = [None] * 8
    for i in range(8):
        value = anchors[first][i & 1]
        for b in (1, 2):
            value = value * anchors[first + b][(i >> b) & 1]
        factors[i] = value
    return factors


def low_table(anchors, first_device, device):
    return low_factor(anchors) * device_factor(anchors, first_device, device)


THETAS, FACTORS, TABLE = 0, 64, 96
PARTS = 1


def table_thetas(table_ref, marker):
    return [table_ref[pl.ds(THETAS + 32 * marker + b, 1), :] for b in range(MEIOSES)]


def emitted(table_ref, low_ref, layout, i, j):
    outer = table_ref[pl.ds(FACTORS + 16 * layout + i, 1), :]
    inner = table_ref[pl.ds(FACTORS + 16 * layout + 8 + j, 1), :]
    return ERROR_RATE + (outer * inner) * low_ref[layout]


def first_kernel(theta_hbm, mask_hbm, fwd_ref, bwd_ref, out_ref, table_ref, low_ref, kron_ref, rows_ref,
                 theta_ref, mask_ref, fwd_in, bwd_in, tmp, small, sems):
    scalars = [
        pltpu.make_async_copy(source, target, small.at[k])
        for k, (source, target) in enumerate(((theta_hbm, theta_ref), (mask_hbm, mask_ref)))
    ]
    for copy in scalars:
        copy.start()
    copies = [
        [pltpu.make_async_copy(source, target, sems.at[which])]
        for which, (source, target) in enumerate(((fwd_ref, fwd_in), (bwd_ref, bwd_in)))
    ]
    for row in copies:
        for copy in row:
            copy.start()
    device = lax.axis_index("state")
    for copy in scalars:
        copy.wait()
    thetas = [theta_list(theta_ref, m) for m in range(2)]
    for m in range(2):
        for b in range(MEIOSES):
            table_ref[pl.ds(THETAS + 32 * m + b, 1), :] = jnp.full((1, LANES), thetas[m][b], F32)
    for layout, (marker, chunk, own) in enumerate(((0, HIGH, MID), (1, MID, HIGH))):
        anchors = anchor_list(mask_ref, marker)
        low_ref[layout] = low_table(anchors, own, device)
        for at, bits in ((0, chunk + 3), (8, chunk)):
            for i, value in enumerate(three_bits(anchors, bits)):
                table_ref[pl.ds(FACTORS + 16 * layout + at + i, 1), :] = jnp.full((1, LANES), value, F32)
    for m in range(2):
        for part, value in enumerate(two_parts(kron_rows(thetas[m][:7]))):
            kron_ref[m, part] = value
        for part, value in enumerate(two_parts(kron_rows(thetas[m][7:14]))):
            rows_ref[m, part] = value
    for part, value in enumerate(two_parts(kron_rows(thetas[1][7:11] + thetas[1][17:20]))):
        rows_ref[2, part] = value
    for row in copies:
        row[0].wait()
    for which, source in enumerate((fwd_in, bwd_in)):
        for p in range(PARTS):
            first = p * 64 // PARTS
            chunks = [source[pl.ds((first + k) * ROWS, ROWS), :] for k in range(64 // PARTS)]
            if which == 1:
                chunks = [
                    chunk * emitted(table_ref, low_ref, 1, (first + k) // 8, k % 8)
                    for k, chunk in enumerate(chunks)
                ]
            chunks = mix_blocks(chunks, kron_ref[which], rows_ref[which])
            for k, chunk in enumerate(chunks):
                tmp[which, first + k] = chunk
        for j in range(8):
            chunks = butterfly([tmp[which, 8 * i + j] for i in range(8)], thetas[which][14:17])
            for i in range(8):
                out_ref[8 * i + j, pl.ds(which * ROWS, ROWS), :] = chunks[i]


def second_kernel(table_ref, in_ref, low_ref, kron_ref, rows_ref, out_ref, tmp):
    thetas = [table_thetas(table_ref, m) for m in range(2)]
    for which in range(2):
        before, after = thetas[which], thetas[1 - which]
        rows = pl.ds(which * ROWS, ROWS)
        for j in range(8):
            chunks = butterfly([in_ref[8 * i + j, rows, :] for i in range(8)], before[20:23])
            for i in range(8):
                tmp[which, 8 * i + j] = chunks[i]
        for p in range(PARTS):
            first = p * 64 // PARTS
            both = []
            for i in range(first // 8, (first + 64 // PARTS) // 8):
                chunks = butterfly([tmp[which, 8 * i + j] for j in range(8)], before[17:20])
                chunks = [chunks[j] * emitted(table_ref, low_ref, 0, i, j) for j in range(8)]
                if which == 1:
                    chunks = butterfly(chunks, after[17:20])
                both += chunks
            if which == 0:
                both = mix_blocks(both, kron_ref[1], rows_ref[2])
            for k, chunk in enumerate(both):
                tmp[which, first + k] = chunk
        for j in range(8):
            chunks = butterfly([tmp[which, 8 * i + j] for i in range(8)], after[20:23])
            for i in range(8):
                out_ref[8 * i + j, rows, :] = chunks[i]


def forward_kernel(table_ref, in_ref, low_ref, out_ref, sum_ref, tmp):
    thetas = table_thetas(table_ref, 1)
    for i in range(8):
        chunks = butterfly([in_ref[8 * i + j, pl.ds(0, ROWS), :] for j in range(8)], thetas[11:14])
        for j in range(8):
            tmp[8 * i + j] = chunks[j]
    acc = jnp.zeros((ROWS, LANES), F32)
    for j in range(8):
        chunks = butterfly([tmp[8 * i + j] for i in range(8)], thetas[14:17])
        for i in range(8):
            value = chunks[i] * emitted(table_ref, low_ref, 1, i, j)
            acc = acc + value
            out_ref[pl.ds((8 * i + j) * ROWS, ROWS), :] = value
    sum_ref[...] = acc[:8] + acc[8:]


def backward_kernel(table_ref, in_ref, kron_ref, rows_ref, out_ref, sum_ref, tmp):
    thetas = table_thetas(table_ref, 0)
    for p in range(PARTS):
        first = p * 64 // PARTS
        chunks = [in_ref[first + k, pl.ds(ROWS, ROWS), :] for k in range(64 // PARTS)]
        for k, chunk in enumerate(mix_blocks(chunks, kron_ref[0], rows_ref[0])):
            tmp[first + k] = chunk
    acc = jnp.zeros((ROWS, LANES), F32)
    for j in range(8):
        chunks = butterfly([tmp[8 * i + j] for i in range(8)], thetas[14:17])
        for i in range(8):
            acc = acc + chunks[i]
            out_ref[pl.ds((8 * i + j) * ROWS, ROWS), :] = chunks[i]
    sum_ref[...] = acc[:8] + acc[8:]


def product_kernel(got_ref, bwd_ref, fsum_ref, bsum_ref, first_ref, _, out_ref, sum_ref, first_in, sem):
    is_first = lax.axis_index("seg") == 0

    @pl.when(is_first)
    def _():
        copy = pltpu.make_async_copy(first_ref, first_in, sem)
        copy.start()
        copy.wait()

    def multiply(left_ref):
        acc = jnp.zeros((8, LANES), F32)
        for i in range(16):
            rows = pl.ds(64 * i, 64)
            value = left_ref[rows, :] * bwd_ref[rows, :]
            out_ref[rows, :] = value
            acc = acc + jnp.sum(value.reshape(8, 8, LANES), axis=0)
        lane = lax.broadcasted_iota(jnp.int32, (1, LANES), 1)
        row = jnp.where(
            lane == 0,
            jnp.sum(fsum_ref[...]),
            jnp.where(lane == 1, jnp.sum(bsum_ref[...]), jnp.sum(acc)),
        )
        sum_ref[...] = jnp.broadcast_to(row[None], sum_ref.shape)

    pl.when(is_first)(lambda: multiply(first_in))
    pl.when(jnp.logical_not(is_first))(lambda: multiply(got_ref))


def scale_kernel(total_ref, fwd_ref, bwd_ref, post_ref, fwd_out, bwd_out, post_out, log_ref, ready, sems):
    totals = jnp.sum(total_ref[...], axis=0)
    means = totals * (1.0 / 2.0**MEIOSES)
    lane = lax.broadcasted_iota(jnp.int32, (1, LANES), 1)
    copies = []
    for which, (source, target) in enumerate(
        ((fwd_ref, fwd_out), (bwd_ref, bwd_out), (post_ref, post_out))
    ):
        mean = jnp.sum(jnp.where(lane == which, means, 0.0), axis=1, keepdims=True)
        scale = 1.0 / mean
        for half in range(2):
            for i in range(4):
                rows = pl.ds(half * 512 + 128 * i, 128)
                ready[which, rows, :] = source[rows, :] * scale
            rows = pl.ds(half * 512, 512)
            copy = pltpu.make_async_copy(
                ready.at[which, rows, :], target.at[rows, :], sems.at[which, half]
            )
            copy.start()
            copies.append(copy)
        if which < 2:
            log_ref[:, pl.ds(which, 1)] = jnp.log(mean)
    for copy in copies:
        copy.wait()


VMEM = pl.BlockSpec(memory_space=pltpu.VMEM)
ANY = pl.BlockSpec(memory_space=pl.ANY)


def kept(array):
    return pltpu.with_memory_space_constraint(array, pltpu.VMEM)


def vmem(*shape, dtype=F32):
    return (VMEM, pltpu.VMEM(shape, dtype))


def exchanged(blocks):
    return lax.all_to_all(blocks, "state", split_axis=0, concat_axis=0, tiled=True)


def call(kernel, name, vectors, raw, outs, scratch=()):
    return pl.pallas_call(
        kernel,
        name=name,
        in_specs=[VMEM] * len(vectors) + [ANY] * len(raw),
        out_specs=[o[0] for o in outs],
        out_shape=[o[1] for o in outs],
        scratch_shapes=scratch,
    )(*[kept(v) for v in vectors], *raw)


def shards(forward_in, backward_in, compat_masks, theta_index):
    groups = lax.axis_size("state")
    pair = (groups, 2 * ROWS, LANES)
    flat = (groups * ROWS, LANES)
    chunk = (groups, ROWS, LANES)
    first = forward_in.reshape(flat)
    both, table, low, kron, rows = call(
        first_kernel,
        "first",
        (),
        (theta_index, compat_masks, first, backward_in.reshape(flat)),
        [
            vmem(*pair),
            vmem(TABLE, LANES),
            vmem(2, ROWS, LANES),
            vmem(2, 2, LANES, LANES, dtype=BF16),
            vmem(3, 2, LANES, LANES, dtype=BF16),
        ],
        [
            pltpu.SMEM(theta_index.shape, jnp.int32),
            pltpu.SMEM(compat_masks.shape, jnp.int32),
            pltpu.VMEM(flat, F32),
            pltpu.VMEM(flat, F32),
            pltpu.VMEM((2, *chunk), F32),
            pltpu.SemaphoreType.DMA((2,)),
            pltpu.SemaphoreType.DMA((2,)),
        ],
    )
    both = exchanged(both)
    (both,) = call(
        second_kernel,
        "second",
        (table, both, low, kron, rows),
        (),
        [vmem(*pair)],
        [pltpu.VMEM((2, *chunk), F32)],
    )
    both = exchanged(both)
    forward, fsum = call(
        forward_kernel,
        "forward",
        (table, both, low),
        (),
        [vmem(*flat), vmem(8, LANES)],
        [pltpu.VMEM(chunk, F32)],
    )
    count = lax.axis_size("seg")
    received = lax.ppermute(forward, "seg", [(s, (s + 1) % count) for s in range(count)])
    backward, bsum = call(
        backward_kernel,
        "backward",
        (table, both, kron, rows),
        (),
        [vmem(*flat), vmem(8, LANES)],
        [pltpu.VMEM(chunk, F32)],
    )
    product, sums = call(
        product_kernel,
        "product",
        (received, backward, fsum, bsum),
        (first, lax.axis_index("seg").reshape(1)),
        [vmem(*flat), vmem(groups, 1, LANES)],
        [pltpu.VMEM(flat, F32), pltpu.SemaphoreType.DMA(())],
    )
    whole = (ANY, jax.ShapeDtypeStruct(flat, F32))
    forward, backward, posterior, logs = call(
        scale_kernel,
        "scale",
        (exchanged(sums), forward, backward, product),
        (),
        [whole, whole, whole, (VMEM, jax.ShapeDtypeStruct((1, 2), F32))],
        [pltpu.VMEM((3, *flat), F32), pltpu.SemaphoreType.DMA((3, 2))],
    )
    return (
        forward.reshape(1, -1),
        backward.reshape(1, -1),
        posterior.reshape(1, -1),
        logs.reshape(2, 1),
    )


def solution(mesh):
    placed = (P("seg", "state"), P("seg", "state"), P("seg", None), P("seg", None))
    return jax.shard_map(
        shards,
        mesh=mesh,
        in_specs=placed,
        out_specs=(P("seg", "state"), P("seg", "state"), P("seg", "state"), P(None, "seg")),
        check_vma=False,
    )
```

```python
import jax
import jax.numpy as jnp
from jax import lax
from jax.experimental import pallas as pl
from jax.experimental.pallas import tpu as pltpu
from jax.sharding import PartitionSpec as P

PENALTY = 0.5
ERROR_RATE = 0.02
BASE_THETA = 0.01
LANE_BITS, LOW_BITS, SPLIT_BITS = 7, 11, 6
ROWS, LANES = 16, 128
MEIOSES = LOW_BITS + 2 * SPLIT_BITS
MID, HIGH = LOW_BITS, LOW_BITS + SPLIT_BITS
F32, BF16 = jnp.float32, jnp.bfloat16


def theta_list(theta_ref, marker):
    return [
        BASE_THETA * lax.shift_left(jnp.int32(1), theta_ref[marker, b]).astype(F32)
        for b in range(MEIOSES)
    ]


def anchor_list(mask_ref, marker):
    pairs = []
    for b in range(MEIOSES):
        mask = mask_ref[marker, b]
        zero = jnp.where(mask & 1 == 1, F32(1.0), F32(PENALTY))
        one = jnp.where(mask >> 1 == 1, F32(1.0), F32(PENALTY))
        pairs.append((zero, one))
    return pairs


def kron_rows(thetas):
    row = lax.broadcasted_iota(jnp.int32, (8, LANES), 0)
    lane = lax.broadcasted_iota(jnp.int32, (8, LANES), 1)
    low = jnp.ones((8, LANES), F32)
    for b in range(3):
        low = low * jnp.where(((row ^ lane) >> b) & 1 == 1, thetas[b], 1.0 - thetas[b])
    pieces = [low]
    for b in range(3, 7):
        bit = (lane >> b) & 1 == 1
        same = jnp.where(bit, thetas[b], 1.0 - thetas[b])
        other = jnp.where(bit, 1.0 - thetas[b], thetas[b])
        pieces = [p * same for p in pieces] + [p * other for p in pieces]
    return jnp.concatenate(pieces, axis=0)


def two_parts(x):
    high = x.astype(BF16)
    return high, (x - high.astype(F32)).astype(BF16)


def mix_lanes(x, kron):
    left = jnp.concatenate(two_parts(x), axis=1)
    once = jnp.concatenate([kron[0], kron[1]], axis=1)
    both = jnp.dot(left, jnp.concatenate([once, once], axis=0), preferred_element_type=F32)
    return both[:, :LANES] + both[:, LANES:]


def mix_row_bits(kron, x):
    right = jnp.concatenate(two_parts(x), axis=0)
    once = jnp.concatenate([kron[0], kron[1]], axis=0)
    both = jnp.dot(jnp.concatenate([once, once], axis=1), right, preferred_element_type=F32)
    return both[:128] + both[128:]


def mix_blocks(chunks, lanes, rows):
    count = len(chunks) // 8
    mixed = mix_lanes(jnp.concatenate(chunks, axis=0), lanes)
    side_by_side = jnp.concatenate([mixed[i * 128 : (i + 1) * 128] for i in range(count)], axis=1)
    mixed = mix_row_bits(rows, side_by_side)
    return [
        mixed[j * ROWS : (j + 1) * ROWS, i * LANES : (i + 1) * LANES]
        for i in range(count)
        for j in range(8)
    ]


def butterfly(values, thetas):
    values = list(values)
    for b, theta in enumerate(thetas):
        step = 1 << b
        for i in range(len(values)):
            if i & step == 0:
                moved = theta * (values[i + step] - values[i])
                values[i], values[i + step] = values[i] + moved, values[i + step] - moved
    return values


def low_factor(anchors):
    row = lax.broadcasted_iota(jnp.int32, (ROWS, LANES), 0)
    lane = lax.broadcasted_iota(jnp.int32, (ROWS, LANES), 1)
    position = row * LANES + lane
    result = jnp.full((ROWS, LANES), 1.0 - ERROR_RATE, F32)
    for b in range(LOW_BITS):
        zero, one = anchors[b]
        result = result * jnp.where((position >> b) & 1 == 1, one, zero)
    return result


def device_factor(anchors, first, device):
    result = F32(1.0)
    for b in range(SPLIT_BITS):
        zero, one = anchors[first + b]
        result = result * jnp.where((device >> b) & 1 == 1, one, zero)
    return result


def three_bits(anchors, first):
    factors = [None] * 8
    for i in range(8):
        value = anchors[first][i & 1]
        for b in (1, 2):
            value = value * anchors[first + b][(i >> b) & 1]
        factors[i] = value
    return factors


def low_table(anchors, first_device, device):
    return low_factor(anchors) * device_factor(anchors, first_device, device)


THETAS, FACTORS, TABLE = 0, 64, 96
PARTS = 1


def table_thetas(table_ref, marker):
    return [table_ref[pl.ds(THETAS + 32 * marker + b, 1), :] for b in range(MEIOSES)]


def emitted(table_ref, low_ref, layout, i, j):
    outer = table_ref[pl.ds(FACTORS + 16 * layout + i, 1), :]
    inner = table_ref[pl.ds(FACTORS + 16 * layout + 8 + j, 1), :]
    return ERROR_RATE + (outer * inner) * low_ref[layout]


def first_kernel(theta_hbm, mask_hbm, fwd_ref, bwd_ref, out_ref, table_ref, low_ref, kron_ref, rows_ref,
                 theta_ref, mask_ref, fwd_in, bwd_in, tmp, small, sems):
    scalars = [
        pltpu.make_async_copy(source, target, small.at[k])
        for k, (source, target) in enumerate(((theta_hbm, theta_ref), (mask_hbm, mask_ref)))
    ]
    for copy in scalars:
        copy.start()
    copies = [
        [pltpu.make_async_copy(source, target, sems.at[which])]
        for which, (source, target) in enumerate(((fwd_ref, fwd_in), (bwd_ref, bwd_in)))
    ]
    for row in copies:
        for copy in row:
            copy.start()
    device = lax.axis_index("state")
    for copy in scalars:
        copy.wait()
    thetas = [theta_list(theta_ref, m) for m in range(2)]
    for m in range(2):
        for b in range(MEIOSES):
            table_ref[pl.ds(THETAS + 32 * m + b, 1), :] = jnp.full((1, LANES), thetas[m][b], F32)
    for layout, (marker, chunk, own) in enumerate(((0, HIGH, MID), (1, MID, HIGH))):
        anchors = anchor_list(mask_ref, marker)
        low_ref[layout] = low_table(anchors, own, device)
        for at, bits in ((0, chunk + 3), (8, chunk)):
            for i, value in enumerate(three_bits(anchors, bits)):
                table_ref[pl.ds(FACTORS + 16 * layout + at + i, 1), :] = jnp.full((1, LANES), value, F32)
    for m in range(2):
        for part, value in enumerate(two_parts(kron_rows(thetas[m][:7]))):
            kron_ref[m, part] = value
        for part, value in enumerate(two_parts(kron_rows(thetas[m][7:14]))):
            rows_ref[m, part] = value
    for part, value in enumerate(two_parts(kron_rows(thetas[1][7:11] + thetas[1][17:20]))):
        rows_ref[2, part] = value
    for row in copies:
        row[0].wait()
    for which, source in enumerate((fwd_in, bwd_in)):
        for p in range(PARTS):
            first = p * 64 // PARTS
            chunks = [source[pl.ds((first + k) * ROWS, ROWS), :] for k in range(64 // PARTS)]
            if which == 1:
                chunks = [
                    chunk * emitted(table_ref, low_ref, 1, (first + k) // 8, k % 8)
                    for k, chunk in enumerate(chunks)
                ]
            chunks = mix_blocks(chunks, kron_ref[which], rows_ref[which])
            for k, chunk in enumerate(chunks):
                tmp[which, first + k] = chunk
        for j in range(8):
            chunks = butterfly([tmp[which, 8 * i + j] for i in range(8)], thetas[which][14:17])
            for i in range(8):
                out_ref[8 * i + j, pl.ds(which * ROWS, ROWS), :] = chunks[i]


def second_kernel(table_ref, in_ref, low_ref, kron_ref, rows_ref, out_ref, tmp):
    thetas = [table_thetas(table_ref, m) for m in range(2)]
    for which in range(2):
        before, after = thetas[which], thetas[1 - which]
        rows = pl.ds(which * ROWS, ROWS)
        for j in range(8):
            chunks = butterfly([in_ref[8 * i + j, rows, :] for i in range(8)], before[20:23])
            for i in range(8):
                tmp[which, 8 * i + j] = chunks[i]
        for p in range(PARTS):
            first = p * 64 // PARTS
            both = []
            for i in range(first // 8, (first + 64 // PARTS) // 8):
                chunks = butterfly([tmp[which, 8 * i + j] for j in range(8)], before[17:20])
                chunks = [chunks[j] * emitted(table_ref, low_ref, 0, i, j) for j in range(8)]
                if which == 1:
                    chunks = butterfly(chunks, after[17:20])
                both += chunks
            if which == 0:
                both = mix_blocks(both, kron_ref[1], rows_ref[2])
            for k, chunk in enumerate(both):
                tmp[which, first + k] = chunk
        for j in range(8):
            chunks = butterfly([tmp[which, 8 * i + j] for i in range(8)], after[20:23])
            for i in range(8):
                out_ref[8 * i + j, rows, :] = chunks[i]


def forward_kernel(table_ref, in_ref, low_ref, out_ref, sum_ref, tmp):
    thetas = table_thetas(table_ref, 1)
    for i in range(8):
        chunks = butterfly([in_ref[8 * i + j, pl.ds(0, ROWS), :] for j in range(8)], thetas[11:14])
        for j in range(8):
            tmp[8 * i + j] = chunks[j]
    acc = jnp.zeros((ROWS, LANES), F32)
    for j in range(8):
        chunks = butterfly([tmp[8 * i + j] for i in range(8)], thetas[14:17])
        for i in range(8):
            value = chunks[i] * emitted(table_ref, low_ref, 1, i, j)
            acc = acc + value
            out_ref[pl.ds((8 * i + j) * ROWS, ROWS), :] = value
    sum_ref[...] = acc[:8] + acc[8:]


def backward_kernel(table_ref, in_ref, kron_ref, rows_ref, first_ref, out_ref, sum_ref, left_ref, tmp, sem):
    copy = pltpu.make_async_copy(first_ref, left_ref, sem)
    copy.start()
    thetas = table_thetas(table_ref, 0)
    for p in range(PARTS):
        first = p * 64 // PARTS
        chunks = [in_ref[first + k, pl.ds(ROWS, ROWS), :] for k in range(64 // PARTS)]
        for k, chunk in enumerate(mix_blocks(chunks, kron_ref[0], rows_ref[0])):
            tmp[first + k] = chunk
    acc = jnp.zeros((ROWS, LANES), F32)
    for j in range(8):
        chunks = butterfly([tmp[8 * i + j] for i in range(8)], thetas[14:17])
        for i in range(8):
            acc = acc + chunks[i]
            out_ref[pl.ds((8 * i + j) * ROWS, ROWS), :] = chunks[i]
    sum_ref[...] = acc[:8] + acc[8:]
    copy.wait()


def product_kernel(got_ref, bwd_ref, fsum_ref, bsum_ref, first_ref, out_ref, sum_ref):
    is_first = lax.axis_index("seg") == 0

    def multiply(left_ref):
        acc = jnp.zeros((8, LANES), F32)
        for i in range(16):
            rows = pl.ds(64 * i, 64)
            value = left_ref[rows, :] * bwd_ref[rows, :]
            out_ref[rows, :] = value
            acc = acc + jnp.sum(value.reshape(8, 8, LANES), axis=0)
        lane = lax.broadcasted_iota(jnp.int32, (1, LANES), 1)
        row = jnp.where(
            lane == 0,
            jnp.sum(fsum_ref[...]),
            jnp.where(lane == 1, jnp.sum(bsum_ref[...]), jnp.sum(acc)),
        )
        sum_ref[...] = jnp.broadcast_to(row[None], sum_ref.shape)

    pl.when(is_first)(lambda: multiply(first_ref))
    pl.when(jnp.logical_not(is_first))(lambda: multiply(got_ref))


def scale_kernel(total_ref, fwd_ref, bwd_ref, post_ref, fwd_out, bwd_out, post_out, log_ref, ready, sems):
    totals = jnp.sum(total_ref[...], axis=0)
    means = totals * (1.0 / 2.0**MEIOSES)
    lane = lax.broadcasted_iota(jnp.int32, (1, LANES), 1)
    copies = []
    for which, (source, target) in enumerate(
        ((fwd_ref, fwd_out), (bwd_ref, bwd_out), (post_ref, post_out))
    ):
        mean = jnp.sum(jnp.where(lane == which, means, 0.0), axis=1, keepdims=True)
        scale = 1.0 / mean
        for half in range(2):
            for i in range(4):
                rows = pl.ds(half * 512 + 128 * i, 128)
                ready[which, rows, :] = source[rows, :] * scale
            rows = pl.ds(half * 512, 512)
            copy = pltpu.make_async_copy(
                ready.at[which, rows, :], target.at[rows, :], sems.at[which, half]
            )
            copy.start()
            copies.append(copy)
        if which < 2:
            log_ref[:, pl.ds(which, 1)] = jnp.log(mean)
    for copy in copies:
        copy.wait()


VMEM = pl.BlockSpec(memory_space=pltpu.VMEM)
ANY = pl.BlockSpec(memory_space=pl.ANY)


def kept(array):
    return pltpu.with_memory_space_constraint(array, pltpu.VMEM)


def vmem(*shape, dtype=F32):
    return (VMEM, pltpu.VMEM(shape, dtype))


def exchanged(blocks):
    return lax.all_to_all(blocks, "state", split_axis=0, concat_axis=0, tiled=True)


def call(kernel, name, vectors, raw, outs, scratch=()):
    raw_in_hbm = len(raw) > 1
    return pl.pallas_call(
        kernel,
        name=name,
        in_specs=[VMEM] * len(vectors) + [ANY] * len(raw),
        out_specs=[o[0] for o in outs],
        out_shape=[o[1] for o in outs],
        scratch_shapes=scratch,
        compiler_params=pltpu.CompilerParams(vmem_limit_bytes=None if raw_in_hbm else 8 << 20),
    )(*[kept(v) for v in vectors], *raw)


def shards(forward_in, backward_in, compat_masks, theta_index):
    groups = lax.axis_size("state")
    pair = (groups, 2 * ROWS, LANES)
    flat = (groups * ROWS, LANES)
    chunk = (groups, ROWS, LANES)
    first = forward_in.reshape(flat)
    both, table, low, kron, rows = call(
        first_kernel,
        "first",
        (),
        (theta_index, compat_masks, first, backward_in.reshape(flat)),
        [
            vmem(*pair),
            vmem(TABLE, LANES),
            vmem(2, ROWS, LANES),
            vmem(2, 2, LANES, LANES, dtype=BF16),
            vmem(3, 2, LANES, LANES, dtype=BF16),
        ],
        [
            pltpu.SMEM(theta_index.shape, jnp.int32),
            pltpu.SMEM(compat_masks.shape, jnp.int32),
            pltpu.VMEM(flat, F32),
            pltpu.VMEM(flat, F32),
            pltpu.VMEM((2, *chunk), F32),
            pltpu.SemaphoreType.DMA((2,)),
            pltpu.SemaphoreType.DMA((2,)),
        ],
    )
    both = exchanged(both)
    (both,) = call(
        second_kernel,
        "second",
        (table, both, low, kron, rows),
        (),
        [vmem(*pair)],
        [pltpu.VMEM((2, *chunk), F32)],
    )
    both = exchanged(both)
    forward, fsum = call(
        forward_kernel,
        "forward",
        (table, both, low),
        (),
        [vmem(*flat), vmem(8, LANES)],
        [pltpu.VMEM(chunk, F32)],
    )
    count = lax.axis_size("seg")
    received = lax.ppermute(forward, "seg", [(s, (s + 1) % count) for s in range(count)])
    backward, bsum, left = call(
        backward_kernel,
        "backward",
        (table, both, kron, rows),
        (first,),
        [vmem(*flat), vmem(8, LANES), vmem(*flat)],
        [pltpu.VMEM(chunk, F32), pltpu.SemaphoreType.DMA(())],
    )
    product, sums = call(
        product_kernel,
        "product",
        (received, backward, fsum, bsum, left),
        (),
        [vmem(*flat), vmem(groups, 1, LANES)],
    )
    whole = (ANY, jax.ShapeDtypeStruct(flat, F32))
    forward, backward, posterior, logs = call(
        scale_kernel,
        "scale",
        (exchanged(sums), forward, backward, product),
        (),
        [whole, whole, whole, (VMEM, jax.ShapeDtypeStruct((1, 2), F32))],
        [pltpu.VMEM((3, *flat), F32), pltpu.SemaphoreType.DMA((3, 2))],
    )
    return (
        forward.reshape(1, -1),
        backward.reshape(1, -1),
        posterior.reshape(1, -1),
        logs.reshape(2, 1),
    )


def solution(mesh):
    placed = (P("seg", "state"), P("seg", "state"), P("seg", None), P("seg", None))
    return jax.shard_map(
        shards,
        mesh=mesh,
        in_specs=placed,
        out_specs=(P("seg", "state"), P("seg", "state"), P("seg", "state"), P(None, "seg")),
        check_vma=False,
    )
```
